512 devices in a mesh: dom: 128 (over x, z, core), rep: 4 (over y).
Axes of the slice: x: 4, y: 4, z: 16, core: 2. Of those that a mesh axis runs over, the one named last changes fastest.
Arguments:
- feats: bfloat16 [524288, 256], P(('dom', 'rep')), may hold values from -6 to 6
- w_self: bfloat16 [256, 256], replicated, may hold values from -0.375 to 0.375
- w_neigh: bfloat16 [256, 256], replicated, may hold values from -0.375 to 0.375
- bias: float32 [256], replicated, may hold values from -3 to 3
- out_cot: bfloat16 [524288, 256], P(('dom', 'rep')), may hold values from -6 to 6
- degree: int32 [524288], P(('dom', 'rep')), may hold values from 1 to 20
- edge_src: int32 [524288, 10], P(('dom', 'rep')), may hold values from 0 to 2559, as said below
- hub_rows: int32 [1024], P(('dom', 'rep')), may hold values from 0 to 1023, as said below
- send_rows: int32 [65536, 4], P(('dom', 'rep')), may hold values from -1 to 1023, as said below
Outputs:
- outputs: bfloat16 [524288, 256], P(('dom', 'rep'))
- grad_feats: bfloat16 [524288, 256], P(('dom', 'rep'))
- unit_w_self: float32 [256, 256], replicated
- unit_w_neigh: float32 [256, 256], replicated
- unit_bias: float32 [256], replicated
The draws below stay inside these ranges and needn't reach their ends.
Inputs may be any that keep to these rules, and one draw needn't show every extreme that they name: `hub_rows`: the 2 entries of one block are distinct rows of that block. `send_rows`: row q * 128 + e lists rows of block q for partition e: live entries first, then -1; every list has a live entry, every block has a full list, and one partition receives full lists from all blocks. `edge_src`: A slot of the halo part of a block's table always names a live entry of the list it comes from.
All inputs are finite; a program needn't handle non-finite values.
Results may differ from the reference program's by a relative error of at most 0.0056.
Values may be sent and summed in bfloat16 or wider, within the bound.
A program may use at most 128 MiB of HBM per device.

```python
import jax
import jax.numpy as jnp
from jax import lax

F = 256
FANOUT = 10
ROWS = 1024
HUB_DEV = 2
CAP = 4
NODES = 524288
HUBS = 1024
N_DOM = 128
N_REP = 4


def halo_plan(key):
    base_key = jax.random.fold_in(key, 7)
    key_counts, key_target, key_busy, key_rows = jax.random.split(base_key, 4)
    block_total = N_DOM * N_REP
    list_counts = jax.random.randint(key_counts, (block_total, N_DOM), 1, CAP + 1)
    target = jax.random.randint(key_target, (block_total, 1), 0, N_DOM)
    busiest = jax.random.randint(key_busy, (1, 1), 0, N_DOM)
    columns = jnp.arange(N_DOM, dtype=jnp.int32)[None, :]
    list_counts = jnp.where((columns == target) | (columns == busiest), CAP, list_counts)
    chosen = jax.random.randint(key_rows, (block_total, N_DOM, CAP), 0, ROWS)
    places = jnp.arange(CAP, dtype=jnp.int32)[None, None, :]
    listed = jnp.where(places < list_counts[:, :, None], chosen, -1)
    return (list_counts, listed)


def draw_send_rows(key, part):
    list_counts, listed = halo_plan(key)
    return listed.reshape(N_DOM * N_REP * N_DOM, CAP).astype(jnp.int32)


def draw_hub_rows(key, part):
    block_keys = jax.random.split(jax.random.fold_in(key, 3), N_DOM * N_REP)
    picked = jax.vmap(lambda one_key: jax.random.permutation(one_key, ROWS)[:HUB_DEV])(block_keys)
    return picked.reshape(-1).astype(jnp.int32)


def draw_edge_src(key, part):
    list_counts, listed = halo_plan(key)
    block_total = N_DOM * N_REP
    incoming = list_counts.reshape(N_DOM, N_REP, N_DOM).transpose(2, 1, 0).reshape(block_total, N_DOM)
    key_kind, key_local, key_first, key_second, key_source, key_place = jax.random.split(jax.random.fold_in(key, 11), 6)
    shape_all = (block_total, ROWS * FANOUT)
    category = jax.random.randint(key_kind, shape_all, 0, 10)
    local_pick = jax.random.randint(key_local, shape_all, 0, ROWS)
    hub_pick = jnp.minimum(jax.random.randint(key_first, shape_all, 0, HUBS), jax.random.randint(key_second, shape_all, 0, HUBS))
    source = jax.random.randint(key_source, shape_all, 0, N_DOM)
    available = jnp.take_along_axis(incoming, source, axis=1)
    position = jax.random.randint(key_place, shape_all, 0, available)
    halo_pick = ROWS + HUBS + source * CAP + position
    slot_ids = jnp.where(category < 6, local_pick, jnp.where(category < 7, ROWS + hub_pick, halo_pick))
    return slot_ids.reshape(block_total * ROWS, FANOUT).astype(jnp.int32)


def place_ends(entries, key, low, largest):
    longest = entries.shape.index(max(entries.shape))
    spots = []
    for shift in (0, 1):
        where = [jax.random.randint(jax.random.fold_in(key, axis), (), 0, length) for axis, length in enumerate(entries.shape)]
        where[longest] = (where[longest] + shift) % entries.shape[longest]
        spots.append(tuple(where))
    return entries.at[spots[0]].set(low).at[spots[1]].set(largest)


def block_scale(key, extent, shards, smallest, largest):
    level = 1.0
    for dim, parts in shards:
        steps = jax.random.uniform(jax.random.fold_in(jax.random.fold_in(key, 6), dim), (parts,), jnp.float32, smallest / len(shards), largest / len(shards))
        level = level * jnp.repeat(jnp.exp(steps), extent[dim] // parts).reshape((-1,) + (1,) * (len(extent) - 1 - dim))
    return level


def bell_draw(stream_key, extent, spread, limit, pieces=(), kind=jnp.bfloat16):
    result = spread * jax.random.normal(stream_key, extent, jnp.float32)
    if pieces:
        result = result * block_scale(stream_key, extent, pieces, -0.22, 0.18)
    return jnp.clip(result, -limit, limit).astype(kind)


def setup_inputs(seed: int = 0) -> dict:
    streams_of = jax.random.split(jax.random.key(seed), 10)
    feats = bell_draw(streams_of[0], (NODES, F), 1.0, 6.0, ((0, 512),))
    w_self = bell_draw(streams_of[1], (F, F), F ** -0.5, 0.375)
    w_neigh = bell_draw(streams_of[2], (F, F), F ** -0.5, 0.375)
    bias = bell_draw(streams_of[3], (F,), 0.5, 3.0, (), jnp.float32)
    out_cot = bell_draw(streams_of[4], (NODES, F), 1.0, 6.0, ((0, 512),))
    degree = place_ends(jax.random.randint(streams_of[5], (NODES,), 1, 2 * FANOUT + 1), jax.random.fold_in(streams_of[5], 1), 1, 2 * FANOUT).astype(jnp.int32)
    edge_src = draw_edge_src(jax.random.fold_in(streams_of[9], 71), 0)
    hub_rows = draw_hub_rows(jax.random.fold_in(streams_of[9], 71), 0)
    send_rows = draw_send_rows(jax.random.fold_in(streams_of[9], 71), 0)
    return {"feats": feats, "w_self": w_self, "w_neigh": w_neigh, "bias": bias, "out_cot": out_cot, "degree": degree, "edge_src": edge_src, "hub_rows": hub_rows, "send_rows": send_rows}


NORM_EPS = 1e-05
UNIT_EPS = 1e-06

def output_head(preact):
    act = jax.nn.elu(preact)
    return act * lax.rsqrt(lax.optimization_barrier(jnp.mean(act * act, axis=-1, keepdims=True)) + NORM_EPS)

def unit_scale(grad):
    return grad * lax.rsqrt(jnp.mean(grad * grad) + UNIT_EPS)

def slot_globals(hub_rows, send_rows):
    block_total = N_DOM * N_REP
    own_nodes = jnp.arange(block_total, dtype=jnp.int32)[:, None] * ROWS + jnp.arange(ROWS, dtype=jnp.int32)[None, :]
    hub_global = jnp.arange(HUBS, dtype=jnp.int32) // HUB_DEV * ROWS + hub_rows
    hub_part = jnp.broadcast_to(hub_global[None, :], (block_total, HUBS))
    listed = send_rows.reshape(N_DOM, N_REP, N_DOM, CAP).transpose(2, 1, 0, 3)
    sender = jnp.arange(N_DOM, dtype=jnp.int32)[None, None, :, None] * N_REP + jnp.arange(N_REP, dtype=jnp.int32)[None, :, None, None]
    halo_part = jnp.where(listed >= 0, sender * ROWS + listed, -1).reshape(block_total, N_DOM * CAP)
    return jnp.concatenate([own_nodes, hub_part, halo_part.astype(jnp.int32)], axis=1)

def reference(feats, w_self, w_neigh, bias, out_cot, degree, edge_src, hub_rows, send_rows):
    block_total = N_DOM * N_REP
    slot_nodes = slot_globals(hub_rows, send_rows)
    picked = jnp.take_along_axis(slot_nodes, edge_src.reshape(block_total, ROWS * FANOUT), axis=1)
    picked = picked.reshape(block_total * ROWS, FANOUT)
    valid_count = jnp.minimum(degree, FANOUT)
    live_mask = (jnp.arange(FANOUT, dtype=jnp.int32)[None, :] < valid_count[:, None]) & (picked >= 0)
    slot_safe = jnp.maximum(picked, 0)
    summed = jnp.zeros((block_total * ROWS, F), jnp.float32)
    for sample in range(FANOUT):
        gathered = feats[slot_safe[:, sample]].astype(jnp.float32)
        summed = summed + jnp.where(live_mask[:, sample:sample + 1], gathered, jnp.float32(0.0))
    divisor = valid_count.astype(jnp.float32)[:, None]
    neighbor_mean = (summed / divisor).astype(jnp.bfloat16)
    preact = jnp.dot(feats, w_self, preferred_element_type=jnp.float32) + jnp.dot(neighbor_mean, w_neigh, preferred_element_type=jnp.float32) + bias
    outputs, backward = jax.vjp(output_head, preact)
    grad_pre, = backward(out_cot.astype(jnp.float32))
    grad_low = grad_pre.astype(jnp.bfloat16)
    grad_w_self = jnp.dot(feats.T, grad_low, preferred_element_type=jnp.float32)
    grad_w_neigh = jnp.dot(neighbor_mean.T, grad_low, preferred_element_type=jnp.float32)
    grad_bias = lax.optimization_barrier(jnp.sum(grad_pre, axis=0))
    feat_grad = jnp.dot(grad_low, w_self.T, preferred_element_type=jnp.float32)
    edge_grad = jnp.dot(grad_low, w_neigh.T, preferred_element_type=jnp.float32) / divisor
    for sample in range(FANOUT):
        feat_grad = feat_grad.at[slot_safe[:, sample]].add(jnp.where(live_mask[:, sample:sample + 1], edge_grad, jnp.float32(0.0)))
    return (outputs.astype(jnp.bfloat16), feat_grad.astype(jnp.bfloat16), unit_scale(grad_w_self), unit_scale(grad_w_neigh), unit_scale(grad_bias))
```

```python
import jax
import jax.numpy as jnp
from jax import lax
from jax.experimental import pallas as pl
from jax.experimental.pallas import tpu as pltpu
from jax.sharding import PartitionSpec as P

NORM_EPS = 1e-05
UNIT_EPS = 1e-06
NX, NZ, NC, NY = 4, 16, 2, 4
NYX = NY * NX
NXC = NX * NC
MESH = pl.DeviceIdType.MESH
F32 = jnp.float32
BF16 = jnp.bfloat16


def coords():
    d = lax.axis_index("dom")
    y = lax.axis_index("rep")
    return d // (NZ * NC), (d // NC) % NZ, d % NC, y


def dev(x, z, c, y):
    return ((x * NZ + z) * NC + c, y)


def z_peers(x, z, c, y):
    return [dev(x, (z + i) % NZ, c, y) for i in range(1, NZ)]


def yx_peers(x, z, c, y):
    return [dev((x + i % NX) % NX, z, c, (y + i // NX) % NY) for i in range(1, NYX)]


def xc_peers(x, z, c, y):
    return [dev((x + i // NC) % NX, z, (c + i % NC) % NC, y) for i in range(1, NXC)]


def entry_barrier_signal(x, z, c, y):
    peers = z_peers(x, z, c, y) + xc_peers(x, z, c, y)
    peers += [p for i, p in enumerate(yx_peers(x, z, c, y), 1) if i // NX != 0]
    barrier = pltpu.get_barrier_semaphore()
    for p in peers:
        pl.semaphore_signal(barrier, inc=1, device_id=p, device_id_type=MESH)
    return barrier, len(peers)


def rcopy(src, dst, ssem, rsem, peer):
    return pltpu.make_async_remote_copy(
        src_ref=src, dst_ref=dst, send_sem=ssem, recv_sem=rsem, device_id=peer, device_id_type=MESH
    )


def pick_kernel(feats_ref, send_ref, hub_ref, out_ref, hub_out_ref):
    rows = feats_ref.shape[0]
    feats = feats_ref[...]
    idx = send_ref[...]
    lane = lax.broadcasted_iota(jnp.int32, (idx.shape[0], rows), 1)
    hot = jnp.where(idx == lane, 1.0, 0.0).astype(BF16)
    out_ref[...] = jnp.dot(hot, feats, preferred_element_type=F32).astype(BF16)
    hidx = hub_ref[...]
    hlane = lax.broadcasted_iota(jnp.int32, (8, rows), 1)
    hhot = jnp.where(hidx == hlane, 1.0, 0.0).astype(BF16)
    hub_out_ref[...] = jnp.dot(hhot, feats, preferred_element_type=F32)[:2]


def fwd_exchange_kernel(s_ref, hub_ref, edge_ref, deg_ref, h_ref, hubtab_ref, a_ref,
                        t_ref, zbuf, z32, eslot,
                        own_sem, x_ss, x_rs, z_ss, z_rs, hz_ss, hz_rs, hp_ss, hp_rs, hc_ss, hc_rs):
    x, z, c, y = coords()
    xc = x * NC + c
    yx = y * NX + x
    barrier, nbar = entry_barrier_signal(x, z, c, y)
    rows, fan = edge_ref.shape
    slots = a_ref.shape[1]
    hubs = 2 * NC * NYX * NZ

    e = edge_ref[...]
    h = e - rows
    hub_pos = ((((h // (2 * NY)) % NC * NY + (h // 2) % NY) * NX + h // (2 * NY * NC * NZ)) * NZ
               + (h // (2 * NY * NC)) % NZ) * 2 + h % 2
    g = h - hubs
    halo_pos = (((g // (4 * NC)) % NZ * NX + g // (4 * NC * NZ)) * NC + (g // 4) % NC) * 4 + g % 4
    pos = jnp.where(e < rows, e, jnp.where(e < rows + hubs, rows + hub_pos, rows + hubs + halo_pos))
    live = lax.broadcasted_iota(jnp.int32, e.shape, 1) < jnp.minimum(deg_ref[...], fan)
    eslot[...] = jnp.where(live, pos, -1)

    step = 16
    tile = min(128, slots)

    def build(lo, hi):
        def body(b, carry):
            r0 = pl.multiple_of(b * step, step)
            ids = eslot[pl.ds(r0, step), :]
            lane = lax.broadcasted_iota(jnp.int32, (step, tile), 1)
            diff = [ids[:, k:k + 1] - lane for k in range(fan)]
            for t in range(slots // tile):
                acc = jnp.zeros((step, tile), F32)
                for k in range(fan):
                    acc = acc + jnp.where(diff[k] == t * tile, 1.0, 0.0)
                a_ref[pl.ds(r0, step), t * tile:(t + 1) * tile] = acc.astype(BF16)
            return carry
        lax.fori_loop(lo, hi, body, 0)

    nblk = rows // step
    cuts = [0, nblk // 8, nblk * 3 // 8, nblk * 6 // 8, nblk]

    own = [pltpu.make_async_copy(s_ref.at[xc], t_ref.at[:, xc], own_sem.at[0]),
           pltpu.make_async_copy(hub_ref, zbuf.at[z], own_sem.at[1])]
    for cp in own:
        cp.start()
    build(cuts[0], cuts[1])
    pl.semaphore_wait(barrier, nbar)

    hz = [rcopy(hub_ref, zbuf.at[z], hz_ss.at[i], hz_rs.at[i], p)
          for i, p in enumerate(z_peers(x, z, c, y))]
    for cp in hz:
        cp.start()
    st1 = []
    for i, p in enumerate(xc_peers(x, z, c, y), 1):
        pxc = ((x + i // NC) % NX) * NC + (c + i % NC) % NC
        st1.append(rcopy(s_ref.at[pxc], t_ref.at[:, xc], x_ss.at[i - 1], x_rs.at[i - 1], p))
    for cp in st1:
        cp.start()
    build(cuts[1], cuts[2])
    for cp in own:
        cp.wait()
    for cp in st1:
        cp.wait_recv()
    own2 = pltpu.make_async_copy(t_ref.at[z], h_ref.at[z], own_sem.at[2])
    own2.start()
    st2 = [rcopy(t_ref.at[(z + i) % NZ], h_ref.at[z], z_ss.at[i - 1], z_rs.at[i - 1], p)
           for i, p in enumerate(z_peers(x, z, c, y), 1)]
    for cp in st2:
        cp.start()
    for cp in hz:
        cp.wait_recv()
    for i in range(NZ):
        z32[2 * i:2 * i + 2, :] = zbuf[i]
    hubtab_ref[c, yx] = z32[...].astype(BF16)
    hp = [rcopy(hubtab_ref.at[c, yx], hubtab_ref.at[c, yx], hp_ss.at[i], hp_rs.at[i], p)
          for i, p in enumerate(yx_peers(x, z, c, y))]
    for cp in hp:
        cp.start()
    build(cuts[2], cuts[3])
    for cp in hp:
        cp.wait_recv()
    hc = rcopy(hubtab_ref.at[c], hubtab_ref.at[c], hc_ss, hc_rs, dev(x, z, 1 - c, y))
    hc.start()
    build(cuts[3], cuts[4])
    hc.wait_recv()
    own2.wait()
    for cp in st2:
        cp.wait_recv()
    for cp in hz + st1 + st2 + hp + [hc]:
        cp.wait_send()


def layer_kernel(feats_ref, hub_ref, halo_ref, a_ref, ws_ref, wn_ref, bias_ref, cot_ref, deg_ref,
                 out_ref, base_ref, hubg_ref, halog_ref, wg_ref, bg_ref, nm_ref, gl_ref, eg_ref):
    rows, width = feats_ref.shape
    nh = hub_ref.shape[0]
    ng = halo_ref.shape[0]
    fan = 10
    nt = (((1,), (1,)), ((), ()))
    tn = (((0,), (0,)), ((), ()))
    blk = min(256, rows)
    bsum = jnp.zeros((1, width), F32)
    for b in range(rows // blk):
        rs = slice(b * blk, (b + 1) * blk)
        summed = jnp.dot(a_ref[rs, :rows], feats_ref[...], preferred_element_type=F32)
        summed += jnp.dot(a_ref[rs, rows:rows + nh], hub_ref[...], preferred_element_type=F32)
        summed += jnp.dot(a_ref[rs, rows + nh:], halo_ref[...], preferred_element_type=F32)
        divisor = jnp.minimum(deg_ref[rs, :], fan).astype(F32)
        nm = (summed / divisor).astype(BF16)
        nm_ref[rs, :] = nm
        pre = (jnp.dot(feats_ref[rs, :], ws_ref[...], preferred_element_type=F32)
               + jnp.dot(nm, wn_ref[...], preferred_element_type=F32) + bias_ref[...])
        ex = jnp.exp(jnp.minimum(pre, 0.0))
        act = jnp.where(pre > 0, pre, ex - 1.0)
        inv = lax.rsqrt(jnp.mean(act * act, axis=-1, keepdims=True) + NORM_EPS)
        out_ref[rs, :] = (act * inv).astype(BF16)
        cot = cot_ref[rs, :].astype(F32)
        dot = jnp.mean(act * cot, axis=-1, keepdims=True)
        gpre = inv * (cot - act * (inv * inv * dot)) * jnp.where(pre > 0, 1.0, ex)
        bsum = bsum + jnp.sum(gpre, axis=0, keepdims=True)
        gl = gpre.astype(BF16)
        gl_ref[rs, :] = gl
        base_ref[rs, :] = lax.dot_general(gl, ws_ref[...], nt, preferred_element_type=F32)
        eg_ref[rs, :] = (lax.dot_general(gl, wn_ref[...], nt, preferred_element_type=F32)
                         / divisor).astype(BF16)
    bg_ref[...] = bsum
    eg = eg_ref[...]
    step = min(512, ng)
    for o in range(0, rows, step):
        base_ref[o:o + step, :] += lax.dot_general(a_ref[:, o:o + step], eg, tn,
                                                   preferred_element_type=F32)
    for o in range(0, nh, step):
        hubg_ref[o:o + step, :] = lax.dot_general(a_ref[:, rows + o:rows + o + step], eg, tn,
                                                  preferred_element_type=F32).astype(BF16)
    for o in range(0, ng, step):
        halog_ref[o:o + step, :] = lax.dot_general(a_ref[:, rows + nh + o:rows + nh + o + step], eg, tn,
                                                   preferred_element_type=F32).astype(BF16)
    gl = gl_ref[...]
    wg_ref[:width, :] = lax.dot_general(feats_ref[...], gl, tn, preferred_element_type=F32).astype(BF16)
    wg_ref[width:, :] = lax.dot_general(nm_ref[...], gl, tn, preferred_element_type=F32).astype(BF16)


def bwd_exchange_kernel(g_ref, hubg_ref, wg_ref, bg_ref, r_ref, own_ref, wfull_ref,
                        t_ref, hubc, wc, bc, hub1, w1, b1, hubp, wp, bp, zsend, zrecv, wz, wrow,
                        own_sem, z_ss, z_rs, x_ss, x_rs, c_ss, c_rs, p_ss, p_rs, q_ss, q_rs,
                        az_ss, az_rs, ap_ss, ap_rs, ac_ss, ac_rs):
    x, z, c, y = coords()
    xc = x * NC + c
    yx = y * NX + x
    barrier, nbar = entry_barrier_signal(x, z, c, y)
    sib = dev(x, z, 1 - c, y)
    own = pltpu.make_async_copy(g_ref.at[z], t_ref.at[z], own_sem.at[0])
    own.start()
    pl.semaphore_wait(barrier, nbar)

    cs = [rcopy(hubg_ref.at[1 - c], hubc, c_ss.at[0], c_rs.at[0], sib),
          rcopy(wg_ref.at[1 - c], wc, c_ss.at[1], c_rs.at[1], sib),
          rcopy(bg_ref, bc, c_ss.at[2], c_rs.at[2], sib)]
    for cp in cs:
        cp.start()
    st1 = [rcopy(g_ref.at[(z + i) % NZ], t_ref.at[z], z_ss.at[i - 1], z_rs.at[i - 1], p)
           for i, p in enumerate(z_peers(x, z, c, y), 1)]
    for cp in st1:
        cp.start()
    for cp in cs:
        cp.wait_recv()
    hub1[...] = (hubg_ref[c].astype(F32) + hubc[...].astype(F32)).astype(BF16)
    w1[...] = (wg_ref[c].astype(F32) + wc[...].astype(F32)).astype(BF16)
    b1[...] = bg_ref[...] + bc[...]
    ps = []
    for i, p in enumerate(yx_peers(x, z, c, y), 1):
        pyx = ((y + i // NX) % NY) * NX + (x + i % NX) % NX
        ps.append(rcopy(hub1.at[pyx], hubp.at[i - 1], p_ss.at[0, i - 1], p_rs.at[0, i - 1], p))
        ps.append(rcopy(w1.at[pyx], wp.at[i - 1], p_ss.at[1, i - 1], p_rs.at[1, i - 1], p))
        ps.append(rcopy(b1, bp.at[i - 1], p_ss.at[2, i - 1], p_rs.at[2, i - 1], p))
    for cp in ps:
        cp.start()
    for cp in ps:
        cp.wait_recv()
    hub = hub1[yx].astype(F32)
    w = w1[yx].astype(F32)
    bias = b1[...]
    for i in range(NYX - 1):
        hub = hub + hubp[i].astype(F32)
        w = w + wp[i].astype(F32)
        bias = bias + bp[i]
    for i in range(NZ):
        zsend[i, 0:2, :] = hub[2 * i:2 * i + 2, :]
        zsend[i, 2:3, :] = w[i:i + 1, :]
        zsend[i, 3:4, :] = bias
    qs = [rcopy(zsend.at[(z + i) % NZ], zrecv.at[i - 1], q_ss.at[i - 1], q_rs.at[i - 1], p)
          for i, p in enumerate(z_peers(x, z, c, y), 1)]
    for cp in qs:
        cp.start()
    for cp in qs:
        cp.wait_recv()
    total = zsend[z]
    for i in range(NZ - 1):
        total = total + zrecv[i]
    own_ref[...] = total
    wrow[...] = total[2:3, :]
    az = [rcopy(wrow, wz.at[z], az_ss.at[i], az_rs.at[i], p)
          for i, p in enumerate(z_peers(x, z, c, y))]
    for cp in az:
        cp.start()
    wz[z] = total[2:3, :]
    own.wait()
    for cp in st1:
        cp.wait_recv()
    own2 = pltpu.make_async_copy(t_ref.at[:, xc], r_ref.at[xc], own_sem.at[1])
    own2.start()
    st2 = []
    for i, p in enumerate(xc_peers(x, z, c, y), 1):
        pxc = ((x + i // NC) % NX) * NC + (c + i % NC) % NC
        st2.append(rcopy(t_ref.at[:, pxc], r_ref.at[xc], x_ss.at[i - 1], x_rs.at[i - 1], p))
    for cp in st2:
        cp.start()
    for cp in az:
        cp.wait_recv()
    for i in range(NZ):
        wfull_ref[c, yx, i:i + 1, :] = wz[i]
    ap = [rcopy(wfull_ref.at[c, yx], wfull_ref.at[c, yx], ap_ss.at[i], ap_rs.at[i], p)
          for i, p in enumerate(yx_peers(x, z, c, y))]
    for cp in ap:
        cp.start()
    for cp in ap:
        cp.wait_recv()
    ac = rcopy(wfull_ref.at[c], wfull_ref.at[c], ac_ss, ac_rs, sib)
    ac.start()
    ac.wait_recv()
    own2.wait()
    for cp in st2:
        cp.wait_recv()
    for cp in cs + st1 + ps + qs + az + st2 + ap + [ac]:
        cp.wait_send()


def final_kernel(base_ref, ret_ref, send_ref, own_ref, hubrow_ref, wfull_ref,
                 grad_ref, us_ref, un_ref, ub_ref):
    rows, width = base_ref.shape
    lists = send_ref.shape[1]
    node = lax.broadcasted_iota(jnp.int32, (rows, lists), 0)
    hot = jnp.where(send_ref[...] == node, 1.0, 0.0).astype(BF16)
    total = base_ref[...] + jnp.dot(hot, ret_ref[...], preferred_element_type=F32)
    row = lax.broadcasted_iota(jnp.int32, (rows, 1), 0)
    for i in range(2):
        total = total + jnp.where(row == hubrow_ref[i], own_ref[i:i + 1, :], 0.0)
    grad_ref[...] = total.astype(BF16)
    for o, ref in ((0, us_ref), (width, un_ref)):
        w = wfull_ref[o:o + width, :]
        ref[...] = w * lax.rsqrt(jnp.mean(w * w) + UNIT_EPS)
    bias = own_ref[3:4, :]
    ub_ref[...] = bias * lax.rsqrt(jnp.mean(bias * bias) + UNIT_EPS)


def vmem():
    return pl.BlockSpec(memory_space=pltpu.VMEM)


def sds(shape, dtype):
    return jax.ShapeDtypeStruct(shape, dtype)


LIMIT = 48 << 20


def on_device(feats, w_self, w_neigh, bias, out_cot, degree, edge_src, hub_rows, send_rows):
    rows, width = feats.shape
    hubs = 2 * NC * NYX * NZ
    halos = 4 * NXC * NZ
    slots = rows + hubs + halos
    dma = pltpu.SemaphoreType.DMA
    send_order = send_rows.reshape(NX, NZ, NC, 4).transpose(0, 2, 1, 3).reshape(halos)
    hub_col = jnp.concatenate([hub_rows, jnp.full((6,), -1, jnp.int32)]).reshape(8, 1)
    deg_col = degree.reshape(rows, 1)

    outgoing, hub_own = pl.pallas_call(
        pick_kernel,
        out_shape=(sds((halos, width), BF16), sds((2, width), F32)),
        in_specs=[vmem()] * 3, out_specs=(vmem(),) * 2,
        compiler_params=pltpu.CompilerParams(vmem_limit_bytes=LIMIT),
    )(feats, send_order.reshape(halos, 1), hub_col)

    halo, hubtab, a = pl.pallas_call(
        fwd_exchange_kernel,
        out_shape=(sds((NZ, NXC, 4, width), BF16), sds((NC, NYX, 2 * NZ, width), BF16),
                   sds((rows, slots), BF16)),
        in_specs=[vmem()] * 4, out_specs=(vmem(),) * 3,
        scratch_shapes=[
            pltpu.VMEM((NZ, NXC, 4, width), BF16), pltpu.VMEM((NZ, 2, width), F32),
            pltpu.VMEM((2 * NZ, width), F32), pltpu.VMEM(edge_src.shape, jnp.int32),
            dma((3,)), dma((NXC - 1,)), dma((NXC - 1,)), dma((NZ - 1,)), dma((NZ - 1,)),
            dma((NZ - 1,)), dma((NZ - 1,)), dma((NYX - 1,)), dma((NYX - 1,)), dma, dma],
        compiler_params=pltpu.CompilerParams(
            collective_id=0, has_side_effects=True, vmem_limit_bytes=LIMIT),
    )(outgoing.reshape(NXC, NZ, 4, width), hub_own, edge_src, deg_col)

    outputs, base, hubg, halog, wg, bg = pl.pallas_call(
        layer_kernel,
        out_shape=(sds((rows, width), BF16), sds((rows, width), F32), sds((hubs, width), BF16),
                   sds((halos, width), BF16), sds((2 * width, width), BF16), sds((1, width), F32)),
        in_specs=[vmem()] * 9, out_specs=(vmem(),) * 6,
        scratch_shapes=[pltpu.VMEM((rows, width), BF16)] * 3,
        compiler_params=pltpu.CompilerParams(vmem_limit_bytes=LIMIT),
    )(feats, hubtab.reshape(hubs, width), halo.reshape(halos, width), a, w_self, w_neigh,
      bias.reshape(1, width), out_cot, deg_col)

    wrows = 2 * width // (NC * NYX)
    assert wrows == NZ
    back, own, wfull = pl.pallas_call(
        bwd_exchange_kernel,
        out_shape=(sds((NXC, NZ, 4, width), BF16), sds((4, width), F32),
                   sds((NC, NYX, wrows, width), F32)),
        in_specs=[vmem()] * 4, out_specs=(vmem(),) * 3,
        scratch_shapes=[
            pltpu.VMEM((NZ, NXC, 4, width), BF16),
            pltpu.VMEM((NYX, 2 * NZ, width), BF16), pltpu.VMEM((NYX, wrows, width), BF16),
            pltpu.VMEM((1, width), F32),
            pltpu.VMEM((NYX, 2 * NZ, width), BF16), pltpu.VMEM((NYX, wrows, width), BF16),
            pltpu.VMEM((1, width), F32),
            pltpu.VMEM((NYX - 1, 2 * NZ, width), BF16), pltpu.VMEM((NYX - 1, wrows, width), BF16),
            pltpu.VMEM((NYX - 1, 1, width), F32),
            pltpu.VMEM((NZ, 4, width), F32), pltpu.VMEM((NZ - 1, 4, width), F32),
            pltpu.VMEM((NZ, 1, width), F32), pltpu.VMEM((1, width), F32),
            dma((2,)), dma((NZ - 1,)), dma((NZ - 1,)), dma((NXC - 1,)), dma((NXC - 1,)),
            dma((3,)), dma((3,)), dma((3, NYX - 1)), dma((3, NYX - 1)),
            dma((NZ - 1,)), dma((NZ - 1,)), dma((NZ - 1,)), dma((NZ - 1,)),
            dma((NYX - 1,)), dma((NYX - 1,)), dma, dma],
        compiler_params=pltpu.CompilerParams(
            collective_id=1, has_side_effects=True, vmem_limit_bytes=LIMIT),
    )(halog.reshape(NZ, NXC, 4, width), hubg.reshape(NC, NYX, 2 * NZ, width),
      wg.reshape(NC, NYX, wrows, width), bg)

    smem = pl.BlockSpec(memory_space=pltpu.SMEM)
    grad, us, un, ub = pl.pallas_call(
        final_kernel,
        out_shape=(sds((rows, width), BF16), sds((width, width), F32), sds((width, width), F32),
                   sds((1, width), F32)),
        in_specs=[vmem()] * 4 + [smem] + [vmem()], out_specs=(vmem(),) * 4,
        compiler_params=pltpu.CompilerParams(vmem_limit_bytes=LIMIT),
    )(base, back.reshape(halos, width), send_order.reshape(1, halos), own, hub_rows,
      wfull.reshape(2 * width, width))
    return outputs, grad, us, un, ub.reshape(width)


def solution(mesh):
    both = ("dom", "rep")
    placed = (P(both, None), P(), P(), P(), P(both, None), P(both), P(both, None), P(both),
              P(both, None))
    return jax.shard_map(
        on_device,
        mesh=mesh,
        in_specs=placed,
        out_specs=(P(both, None), P(both, None), P(), P(), P()),
        check_vma=False,
    )
```

```python
import jax
import jax.numpy as jnp
from jax import lax
from jax.experimental import pallas as pl
from jax.experimental.pallas import tpu as pltpu
from jax.sharding import PartitionSpec as P

NORM_EPS = 1e-05
UNIT_EPS = 1e-06
NX, NZ, NC, NY = 4, 16, 2, 4
NYX = NY * NX
NXC = NX * NC
MESH = pl.DeviceIdType.MESH
F32 = jnp.float32
BF16 = jnp.bfloat16


def coords():
    d = lax.axis_index("dom")
    y = lax.axis_index("rep")
    return d // (NZ * NC), (d // NC) % NZ, d % NC, y


def dev(x, z, c, y):
    return ((x * NZ + z) * NC + c, y)


def z_offsets():
    return [NZ // 2 - (j + 1) // 2 if j % 2 else NZ // 2 + j // 2 for j in range(NZ)]


def z_slot(i):
    return jnp.where(i >= NZ // 2, 2 * (i - NZ // 2), NZ - 1 - 2 * i)


def z_peers(x, z, c, y):
    return [dev(x, (z + i) % NZ, c, y) for i in range(1, NZ)]


def yx_peers(x, z, c, y):
    return [dev((x + i % NX) % NX, z, c, (y + i // NX) % NY) for i in range(1, NYX)]


def xc_peers(x, z, c, y):
    return [dev((x + i // NC) % NX, z, (c + i % NC) % NC, y) for i in range(1, NXC)]


def entry_barrier_signal(x, z, c, y):
    peers = z_peers(x, z, c, y) + xc_peers(x, z, c, y)
    peers += [p for i, p in enumerate(yx_peers(x, z, c, y), 1) if i // NX != 0]
    barrier = pltpu.get_barrier_semaphore()
    for p in peers:
        pl.semaphore_signal(barrier, inc=1, device_id=p, device_id_type=MESH)
    return barrier, len(peers)


def rcopy(src, dst, ssem, rsem, peer):
    return pltpu.make_async_remote_copy(
        src_ref=src, dst_ref=dst, send_sem=ssem, recv_sem=rsem, device_id=peer, device_id_type=MESH
    )


TN = (((0,), (0,)), ((), ()))
NT = (((1,), (1,)), ((), ()))


def hot_nodes(send_ref, rows):
    lists = send_ref.shape[1]
    node = lax.broadcasted_iota(jnp.int32, (rows, lists), 0)
    return jnp.concatenate(
        [jnp.where(send_ref[k:k + 1, :] == node, 1.0, 0.0).astype(BF16)
         for k in range(send_ref.shape[0])], axis=1)


def layer_kernel(feats_hbm, ws_hbm, wn_hbm, cot_hbm, bias_ref, deg_ref, edge_ref, send_ref, hub_ref,
                 out_ref, base_ref, ret_ref, hubown_ref, btot_ref, wfull_ref,
                 fv, wsv, wnv, cotv, eslot, at, s_ref, hown, t_ref, zbuf, z32, hubtab, h_ref,
                 acc, pre0, dvs, nmv, glv, egv,
                 g_ref, t2, hubg, wg, bg, hubc, wc, bc, hub1, w1, b1, hubp, wp, bp,
                 wz_s, wz_r, bz_s, bz_r, hz_s, hz_r,
                 in_sem, own_sem, x_ss, x_rs, z_ss, z_rs, hz_ss, hz_rs, hp_ss, hp_rs, hc_ss, hc_rs,
                 gz_ss, gz_rs, gx_ss, gx_rs, c_ss, c_rs, p_ss, p_rs, q_ss, q_rs,
                 ap_ss, ap_rs, ac_ss, ac_rs):
    x, z, c, y = coords()
    xc = x * NC + c
    yx = y * NX + x
    sib = dev(x, z, 1 - c, y)
    offs = z_offsets()
    zp = [((z + i) % NZ, dev(x, (z + i) % NZ, c, y)) for i in offs[:-1]]
    xcp = [(((x + i // NC) % NX) * NC + (c + i % NC) % NC, p)
           for i, p in enumerate(xc_peers(x, z, c, y), 1)]
    yxp = [(((y + i // NX) % NY) * NX + (x + i % NX) % NX, p)
           for i, p in enumerate(yx_peers(x, z, c, y), 1)]
    barrier, nbar = entry_barrier_signal(x, z, c, y)
    started = []

    def go(cps):
        for cp in cps:
            cp.start()
        started.extend(cps)
        return cps

    def arrive(cps):
        for cp in cps:
            cp.wait_recv()

    rows, width = fv.shape
    fan = edge_ref.shape[0]
    slots = at.shape[0]
    hubs = 2 * NC * NYX * NZ
    halos = 4 * NXC * NZ
    loads = [pltpu.make_async_copy(src, dst, in_sem.at[i]) for i, (src, dst) in enumerate(
        ((feats_hbm, fv), (ws_hbm, wsv), (wn_hbm, wnv), (cot_hbm, cotv)))]
    for cp in loads:
        cp.start()

    hot = hot_nodes(send_ref, rows)
    nhz = NZ // 2
    p = lax.broadcasted_iota(jnp.int32, (halos, halos), 0)
    q = lax.broadcasted_iota(jnp.int32, (halos, halos), 1)
    pxc = (p // (4 * nhz)) % NXC
    want = ((p % 4) * (NXC * NZ)
            + ((pxc // NC) * NZ + 2 * ((p // 4) % nhz) + p // (4 * nhz * NXC)) * NC + pxc % NC)
    perm = jnp.where(q == want, 1.0, 0.0).astype(BF16)
    loads[0].wait()
    picked = lax.dot_general(hot, fv[...], TN, preferred_element_type=F32).astype(BF16)
    picked = jnp.dot(perm, picked, preferred_element_type=F32)
    s_ref[...] = picked.reshape(2, NXC, nhz, 4, width).astype(BF16)
    sub = lax.broadcasted_iota(jnp.int32, (8, rows), 0)
    hrow = jnp.where(sub == 0, hub_ref[0], jnp.where(sub == 1, hub_ref[1], -1))
    hhot = jnp.where(hrow == lax.broadcasted_iota(jnp.int32, (8, rows), 1), 1.0, 0.0).astype(BF16)
    hown[...] = jnp.dot(hhot, fv[...], preferred_element_type=F32)[:2]

    e = edge_ref[...]
    h = e - rows
    hub_pos = ((((h // (2 * NY)) % NC * NY + (h // 2) % NY) * NX + h // (2 * NY * NC * NZ)) * NZ
               + (h // (2 * NY * NC)) % NZ) * 2 + h % 2
    g = h - hubs
    halo_pos = (((g // (4 * NC)) % NZ * NX + g // (4 * NC * NZ)) * NC + (g // 4) % NC) * 4 + g % 4
    pos = jnp.where(e < rows, e, jnp.where(e < rows + hubs, rows + hub_pos, rows + hubs + halo_pos))
    count = jnp.minimum(deg_ref[...], fan)
    live = lax.broadcasted_iota(jnp.int32, e.shape, 0) < count
    eslot[...] = jnp.where(live, pos, -1)
    dvs[...] = lax.dot_general(jnp.where(live, 1.0, 0.0).astype(BF16), jnp.ones((fan, width), BF16),
                               TN, preferred_element_type=F32)

    nb = 128 if rows % 128 == 0 else 64
    i16 = jnp.int16

    def build(lo, hi):
        def body(j, carry):
            c0 = pl.multiple_of(j * nb, nb)
            sl = lax.broadcasted_iota(jnp.int32, (16, nb), 0)
            diff = [(jnp.broadcast_to(eslot[k:k + 1, pl.ds(c0, nb)], (16, nb)) - sl).astype(i16)
                    for k in range(fan)]
            for t in range(slots // 16):
                tot = None
                for k in range(fan):
                    one = jnp.where(diff[k] == i16(t * 16), BF16(1.0), BF16(0.0))
                    tot = one if tot is None else tot + one
                at[t * 16:(t + 1) * 16, pl.ds(c0, nb)] = tot
            return carry
        lax.fori_loop(lo, hi, body, 0)

    nblk = rows // nb
    cuts = [0, nblk * 3 // 8, nblk * 5 // 8, nblk]

    zb = pltpu.make_async_copy(hown, zbuf.at[z], own_sem.at[0])
    zb.start()
    parts = [(z + m) % 2 for m in (0, 1)]
    own1 = [pltpu.make_async_copy(s_ref.at[par, xc], t_ref.at[par, :, xc], own_sem.at[1 + m])
            for m, par in enumerate(parts)]
    for cp in own1:
        cp.start()
    build(cuts[0], cuts[1])
    pl.semaphore_wait(barrier, nbar)
    st1 = [go([rcopy(s_ref.at[par, k], t_ref.at[par, :, xc], x_ss.at[m, i], x_rs.at[m, i], d)
               for i, (k, d) in enumerate(xcp)]) for m, par in enumerate(parts)]
    hz = go([rcopy(hown, zbuf.at[z], hz_ss.at[i], hz_rs.at[i], d) for i, (k, d) in enumerate(zp)])
    build(cuts[1], cuts[2])
    st2 = []
    own2 = pltpu.make_async_copy(t_ref.at[z % 2, z // 2], h_ref.at[z], own_sem.at[3])
    for m in (0, 1):
        own1[m].wait()
        arrive(st1[m])
        st2 += go([rcopy(t_ref.at[k % 2, k // 2], h_ref.at[z], z_ss.at[j], z_rs.at[j], d)
                   for j, (k, d) in enumerate(zp) if offs[j] % 2 == m])
        if m == 0:
            own2.start()
    zb.wait()
    arrive(hz)
    for i in range(NZ):
        z32[2 * i:2 * i + 2, :] = zbuf[i]
    hubtab[c, yx] = z32[...].astype(BF16)
    hp = go([rcopy(hubtab.at[c, yx], hubtab.at[c, yx], hp_ss.at[i], hp_rs.at[i], d)
             for i, (k, d) in enumerate(yxp)])
    build(cuts[2], cuts[3])
    arrive(hp)
    hc = go([rcopy(hubtab.at[c], hubtab.at[c], hc_ss, hc_rs, sib)])
    for cp in loads[1:]:
        cp.wait()
    blk = min(256, rows)
    spans = [slice(b * blk, (b + 1) * blk) for b in range(rows // blk)]
    for rs in spans:
        acc[rs, :] = lax.dot_general(at[:rows, rs], fv[...], TN, preferred_element_type=F32)
        pre0[rs, :] = jnp.dot(fv[rs, :], wsv[...], preferred_element_type=F32) + bias_ref[...]
    arrive(hc)
    hub_rows = hubtab[...].reshape(hubs, width)
    for rs in spans:
        acc[rs, :] += lax.dot_general(at[rows:rows + hubs, rs], hub_rows, TN,
                                      preferred_element_type=F32)
    own2.wait()
    arrive(st2)

    halo = h_ref[...].reshape(halos, width)
    bsum = jnp.zeros((1, width), F32)
    for rs in spans:
        summed = acc[rs, :] + lax.dot_general(at[rows + hubs:, rs], halo, TN,
                                              preferred_element_type=F32)
        nm = (summed / dvs[rs, :]).astype(BF16)
        nmv[rs, :] = nm
        pre = pre0[rs, :] + jnp.dot(nm, wnv[...], preferred_element_type=F32)
        ex = jnp.exp(jnp.minimum(pre, 0.0))
        act = jnp.where(pre > 0, pre, ex - 1.0)
        inv = lax.rsqrt(jnp.mean(act * act, axis=-1, keepdims=True) + NORM_EPS)
        out_ref[rs, :] = (act * inv).astype(BF16)
        cot = cotv[rs, :].astype(F32)
        dot = jnp.mean(act * cot, axis=-1, keepdims=True)
        gpre = inv * (cot - act * (inv * inv * dot)) * jnp.where(pre > 0, 1.0, ex)
        bsum = bsum + jnp.sum(gpre, axis=0, keepdims=True)
        glv[rs, :] = gpre.astype(BF16)
    bg[...] = bsum
    gl = glv[...]
    wrows = wg.shape[1] * wg.shape[2]
    wpart = jnp.concatenate(
        [lax.dot_general(fv[...], gl, TN, preferred_element_type=F32),
         lax.dot_general(nmv[...], gl, TN, preferred_element_type=F32)], axis=0)
    wg[...] = wpart.reshape(wg.shape).astype(BF16)
    cw = go([rcopy(wg.at[1 - c], wc, c_ss.at[0], c_rs.at[0], sib),
             rcopy(bg, bc, c_ss.at[1], c_rs.at[1], sib)])
    for rs in spans:
        egv[rs, :] = (lax.dot_general(glv[rs, :], wnv[...], NT, preferred_element_type=F32)
                      / dvs[rs, :]).astype(BF16)
    eg = egv[...]

    halo_grad = jnp.dot(at[rows + hubs:, :], eg, preferred_element_type=F32)
    g_ref[...] = halo_grad.reshape(NZ, NXC, 4, width).astype(BF16)
    own3 = pltpu.make_async_copy(g_ref.at[z], t2.at[NZ - 1], own_sem.at[4])
    own3.start()
    gz = go([rcopy(g_ref.at[k], t2.at[j], gz_ss.at[j], gz_rs.at[j], d)
             for j, (k, d) in enumerate(zp)])
    arrive(cw)
    w1[...] = (wg[c].astype(F32) + wc[...].astype(F32)).astype(BF16)
    b1[...] = bg[...] + bc[...]
    pw = []
    for i, (k, d) in enumerate(yxp):
        pw += go([rcopy(w1.at[k], wp.at[i], p_ss.at[0, i], p_rs.at[0, i], d),
                  rcopy(b1, bp.at[i], p_ss.at[1, i], p_rs.at[1, i], d)])
    hub_grad = jnp.dot(at[rows:rows + hubs, :], eg, preferred_element_type=F32)
    hubg[...] = hub_grad.reshape(hubg.shape).astype(BF16)
    ch = go([rcopy(hubg.at[1 - c], hubc, c_ss.at[2], c_rs.at[2], sib)])
    arrive(ch)
    hub1[...] = (hubg[c].astype(F32) + hubc[...].astype(F32)).astype(BF16)
    ph = go([rcopy(hub1.at[k], hubp.at[i], p_ss.at[2, i], p_rs.at[2, i], d)
             for i, (k, d) in enumerate(yxp)])
    arrive(pw)
    w = w1[yx].astype(F32)
    bias = b1[...]
    for i in range(NYX - 1):
        w = w + wp[i].astype(F32)
        bias = bias + bp[i]
    wz_s[...] = w.astype(BF16)
    bz_s[...] = bias
    zw = []
    for j, (k, d) in enumerate(zp):
        zw += go([rcopy(wz_s, wz_r.at[j], q_ss.at[0, j], q_rs.at[0, j], d),
                  rcopy(bz_s, bz_r.at[j], q_ss.at[1, j], q_rs.at[1, j], d)])
    base_ref[...] = (lax.dot_general(gl, wsv[...], NT, preferred_element_type=F32)
                     + jnp.dot(at[:rows, :], eg, preferred_element_type=F32))
    arrive(ph)
    hub = hub1[yx].astype(F32)
    for i in range(NYX - 1):
        hub = hub + hubp[i].astype(F32)
    for i in range(NZ):
        hz_s[i] = hub[2 * i:2 * i + 2, :]
    zh = go([rcopy(hz_s.at[k], hz_r.at[j], q_ss.at[2, j], q_rs.at[2, j], d)
             for j, (k, d) in enumerate(zp)])
    half = NZ // 2
    gx = []
    own4 = []
    for m in (0, 1):
        arrive(gz[m * half:(m + 1) * half])
        if m:
            own3.wait()
        part = pl.ds(m * half, half)
        cp = pltpu.make_async_copy(t2.at[part, xc], ret_ref.at[xc, part], own_sem.at[5 + m])
        cp.start()
        own4.append(cp)
        gx += go([rcopy(t2.at[part, k], ret_ref.at[xc, part], gx_ss.at[m, i], gx_rs.at[m, i], d)
                  for i, (k, d) in enumerate(xcp)])
    arrive(zw)
    w = wz_s[...].astype(F32)
    bias = bz_s[...]
    for j in range(NZ - 1):
        w = w + wz_r[j].astype(F32)
        bias = bias + bz_r[j]
    btot_ref[...] = bias
    wfull_ref[c, yx] = w.astype(BF16)
    ap = go([rcopy(wfull_ref.at[c, yx], wfull_ref.at[c, yx], ap_ss.at[i], ap_rs.at[i], d)
             for i, (k, d) in enumerate(yxp)])
    arrive(zh)
    own = hz_s[z]
    for j in range(NZ - 1):
        own = own + hz_r[j]
    hubown_ref[...] = own
    arrive(ap)
    ac = go([rcopy(wfull_ref.at[c], wfull_ref.at[c], ac_ss, ac_rs, sib)])
    for cp in own4:
        cp.wait()
    arrive(gx)
    arrive(ac)
    for cp in started:
        cp.wait_send()


def final_kernel(base_ref, ret_ref, send_ref, own_ref, hubrow_ref, btot_ref, wfull_ref,
                 grad_ref, us_ref, un_ref, ub_ref):
    rows, width = base_ref.shape
    halos = 4 * NXC * NZ
    z = coords()[1]
    p = lax.broadcasted_iota(jnp.int32, (halos, halos), 0)
    q = lax.broadcasted_iota(jnp.int32, (halos, halos), 1)
    e = p % (NXC * NZ)
    back = (z - (e // NC) % NZ + NZ) % NZ
    want = ((((e // (NC * NZ)) * NC + e % NC) * NZ) + z_slot(back)) * 4 + p // (NXC * NZ)
    perm = jnp.where(q == want, 1.0, 0.0).astype(BF16)
    ret = ret_ref[...].reshape(halos, width)
    ret = jnp.dot(perm, ret, preferred_element_type=F32).astype(BF16)
    total = base_ref[...] + jnp.dot(hot_nodes(send_ref, rows), ret, preferred_element_type=F32)
    row = lax.broadcasted_iota(jnp.int32, (rows, 1), 0)
    for i in range(2):
        total = total + jnp.where(row == hubrow_ref[i], own_ref[i:i + 1, :], 0.0)
    grad_ref[...] = total.astype(BF16)
    w = wfull_ref[...].reshape(2 * width, width).astype(F32)
    for o, ref in ((0, us_ref), (width, un_ref)):
        part = w[o:o + width, :]
        ref[...] = part * lax.rsqrt(jnp.mean(part * part) + UNIT_EPS)
    bias = btot_ref[...]
    ub_ref[...] = bias * lax.rsqrt(jnp.mean(bias * bias) + UNIT_EPS)


def vmem():
    return pl.BlockSpec(memory_space=pltpu.VMEM)


def sds(shape, dtype):
    return jax.ShapeDtypeStruct(shape, dtype)


LIMIT = 56 << 20


def on_device(feats, w_self, w_neigh, bias, out_cot, degree, edge_src, hub_rows, send_rows):
    rows, width = feats.shape
    hubs = 2 * NC * NYX * NZ
    halos = 4 * NXC * NZ
    slots = rows + hubs + halos
    fan = edge_src.shape[1]
    wrows = 2 * width // (NC * NYX)
    nhz = NZ // 2
    dma = pltpu.SemaphoreType.DMA
    smem = pl.BlockSpec(memory_space=pltpu.SMEM)
    hbm = pl.BlockSpec(memory_space=pl.ANY)

    def vb(*shape):
        return pltpu.VMEM(shape, BF16)

    def vf(*shape):
        return pltpu.VMEM(shape, F32)

    send_t = send_rows.T
    outputs, base, ret, hubown, btot, wfull = pl.pallas_call(
        layer_kernel,
        out_shape=(sds((rows, width), BF16), sds((rows, width), F32), sds((NXC, NZ, 4, width), BF16),
                   sds((2, width), F32), sds((1, width), F32), sds((NC, NYX, wrows, width), BF16)),
        in_specs=[hbm] * 4 + [vmem()] * 4 + [smem], out_specs=(vmem(),) * 6,
        scratch_shapes=[
            vb(rows, width), vb(width, width), vb(width, width), vb(rows, width),
            pltpu.VMEM((fan, rows), jnp.int32), vb(slots, rows),
            vb(2, NXC, nhz, 4, width), vf(2, width), vb(2, nhz, NXC, 4, width), vf(NZ, 2, width),
            vf(2 * NZ, width), vb(NC, NYX, 2 * NZ, width), vb(NZ, NXC, 4, width),
            vf(rows, width), vf(rows, width), vf(rows, width),
            vb(rows, width), vb(rows, width), vb(rows, width),
            vb(NZ, NXC, 4, width), vb(NZ, NXC, 4, width),
            vb(NC, NYX, 2 * NZ, width), vb(NC, NYX, wrows, width), vf(1, width),
            vb(NYX, 2 * NZ, width), vb(NYX, wrows, width), vf(1, width),
            vb(NYX, 2 * NZ, width), vb(NYX, wrows, width), vf(1, width),
            vb(NYX - 1, 2 * NZ, width), vb(NYX - 1, wrows, width), vf(NYX - 1, 1, width),
            vb(wrows, width), vb(NZ - 1, wrows, width), vf(1, width), vf(NZ - 1, 1, width),
            vf(NZ, 2, width), vf(NZ - 1, 2, width),
            dma((4,)), dma((7,)), dma((2, NXC - 1)), dma((2, NXC - 1)), dma((NZ - 1,)), dma((NZ - 1,)),
            dma((NZ - 1,)), dma((NZ - 1,)), dma((NYX - 1,)), dma((NYX - 1,)), dma, dma,
            dma((NZ - 1,)), dma((NZ - 1,)), dma((2, NXC - 1)), dma((2, NXC - 1)),
            dma((3,)), dma((3,)), dma((3, NYX - 1)), dma((3, NYX - 1)),
            dma((3, NZ - 1)), dma((3, NZ - 1)),
            dma((NYX - 1,)), dma((NYX - 1,)), dma, dma],
        compiler_params=pltpu.CompilerParams(
            collective_id=0, has_side_effects=True, vmem_limit_bytes=LIMIT),
    )(feats, w_self, w_neigh, out_cot, bias.reshape(1, width), degree.reshape(1, rows), edge_src.T,
      send_t, hub_rows)

    grad, us, un, ub = pl.pallas_call(
        final_kernel,
        out_shape=(sds((rows, width), BF16), sds((width, width), F32), sds((width, width), F32),
                   sds((1, width), F32)),
        in_specs=[vmem()] * 4 + [smem] + [vmem()] * 2, out_specs=(vmem(),) * 4,
        compiler_params=pltpu.CompilerParams(vmem_limit_bytes=LIMIT),
    )(base, ret, send_t, hubown, hub_rows, btot, wfull)
    return outputs, grad, us, un, ub.reshape(width)


def solution(mesh):
    both = ("dom", "rep")
    placed = (P(both, None), P(), P(), P(), P(both, None), P(both), P(both, None), P(both),
              P(both, None))
    return jax.shard_map(
        on_device,
        mesh=mesh,
        in_specs=placed,
        out_specs=(P(both, None), P(both, None), P(), P(), P()),
        check_vma=False,
    )
```

```python
import jax
import jax.numpy as jnp
from jax import lax
from jax.experimental import pallas as pl
from jax.experimental.pallas import tpu as pltpu
from jax.sharding import PartitionSpec as P

NORM_EPS = 1e-05
UNIT_EPS = 1e-06
NX, NZ, NC, NY = 4, 16, 2, 4
NZL = 4
NYX = NY * NX
NXC = NX * NC
MESH = pl.DeviceIdType.MESH
F32 = jnp.float32
BF16 = jnp.bfloat16


def coords():
    d = lax.axis_index("dom")
    y = lax.axis_index("rep")
    return d // (NZ * NC), (d // NC) % NZ, d % NC, y


def dev(x, z, c, y):
    return ((x * NZ + z) * NC + c, y)


def z_offsets():
    return [NZ // 2 - (j + 1) // 2 if j % 2 else NZ // 2 + j // 2 for j in range(NZ)]


def z_peers(x, z, c, y):
    return [dev(x, (z + i) % NZ, c, y) for i in range(1, NZ)]


def yx_peers(x, z, c, y):
    return [dev((x + i % NX) % NX, z, c, (y + i // NX) % NY) for i in range(1, NYX)]


def xc_peers(x, z, c, y):
    return [dev((x + i // NC) % NX, z, (c + i % NC) % NC, y) for i in range(1, NXC)]


def entry_barrier_signal(x, z, c, y):
    peers = z_peers(x, z, c, y) + xc_peers(x, z, c, y)
    peers += [p for i, p in enumerate(yx_peers(x, z, c, y), 1) if i // NX != 0]
    barrier = pltpu.get_barrier_semaphore()
    for p in peers:
        pl.semaphore_signal(barrier, inc=1, device_id=p, device_id_type=MESH)
    return barrier, len(peers)


def rcopy(src, dst, ssem, rsem, peer):
    return pltpu.make_async_remote_copy(
        src_ref=src, dst_ref=dst, send_sem=ssem, recv_sem=rsem, device_id=peer, device_id_type=MESH
    )


TN = (((0,), (0,)), ((), ()))
NT = (((1,), (1,)), ((), ()))


def list_ids(send_ref, want):
    ids = send_ref[...]
    places, lists = ids.shape
    n = want.shape[1]
    pick = jnp.where(lax.broadcasted_iota(jnp.int32, (lists, n), 0) == want, 1.0, 0.0).astype(BF16)
    hi = jnp.dot((ids >> 5).astype(F32).astype(BF16), pick, preferred_element_type=F32)
    lo = jnp.dot((ids & 31).astype(F32).astype(BF16), pick, preferred_element_type=F32)
    place = lax.broadcasted_iota(jnp.int32, (places, n), 1) & 3
    mine = place == lax.broadcasted_iota(jnp.int32, (places, n), 0)
    return jnp.sum(jnp.where(mine, hi * 32.0 + lo, 0.0), axis=0, keepdims=True).astype(jnp.int32)


def list_ids_column(send_ref, want):
    ids = send_ref[...]
    places, lists = ids.shape
    n = want.shape[0]
    pick = jnp.where(lax.broadcasted_iota(jnp.int32, (n, lists), 1) == want, 1.0, 0.0).astype(BF16)
    both = jnp.concatenate([ids >> 5, ids & 31], axis=0).astype(F32).astype(BF16)
    got = lax.dot_general(pick, both, NT, preferred_element_type=F32)
    lane = lax.broadcasted_iota(jnp.int32, got.shape, 1)
    mine = (lax.broadcasted_iota(jnp.int32, got.shape, 0) & 3) == (lane & 3)
    got = jnp.where(lane < places, got * 32.0, got)
    return jnp.sum(jnp.where(mine, got, 0.0), axis=1, keepdims=True).astype(jnp.int32)


def div(v, n):
    return v >> (n.bit_length() - 1)


def mod(v, n):
    return v & (n - 1)


def hot_nodes(ids, rows):
    node = lax.broadcasted_iota(jnp.int32, (rows, 128 if ids.shape[1] % 128 == 0 else ids.shape[1]), 0)
    w = node.shape[1]
    return jnp.concatenate(
        [jnp.where(ids[:, o:o + w] == node, 1.0, 0.0).astype(BF16) for o in range(0, ids.shape[1], w)],
        axis=1)


class Exchange:
    def __init__(self, s0, s1, u, v, h, sems):
        self.s0, self.s1, self.u, self.v, self.h = s0, s1, u, v, h
        (self.own, self.ass, self.ars, self.bss, self.brs, self.css, self.crs, self.dss,
         self.drs) = sems
        self.x, self.z, self.c, self.y = coords()
        self.xc = self.x * NC + self.c
        x, z, c, y = self.x, self.z, self.c, self.y
        self.offs = z_offsets()
        self.zp = [((z + i) % NZ, dev(x, (z + i) % NZ, c, y)) for i in self.offs[:-1]]
        self.a = [rcopy(s0.at[k], u.at[z], self.ass.at[j], self.ars.at[j], d)
                  for j, (k, d) in enumerate(self.zp)]
        self.a_own = pltpu.make_async_copy(s0.at[z], u.at[z], self.own.at[0])
        self.cc = [rcopy(v.at[k], h.at[z], self.css.at[j], self.crs.at[j], d)
                   for j, (k, d) in enumerate(self.zp)]
        self.c_own = pltpu.make_async_copy(v.at[z], h.at[z], self.own.at[1])
        self.b = [rcopy(s1.at[(x + i) % NX], v.at[:, self.xc], self.bss.at[i],
                        self.brs.at[NC * i + c], dev((x + i) % NX, z, 1, y)) for i in range(NX)]
        self.b_own = pltpu.make_async_copy(s1.at[x], v.at[:, self.xc], self.own.at[2])
        self.d = [rcopy(u.at[:, (x + i) % NX], h.at[:, self.xc], self.dss.at[i],
                        self.drs.at[NC * i + c], dev((x + i) % NX, z, 0, y)) for i in range(NX)]
        self.d_own = pltpu.make_async_copy(u.at[:, x], h.at[:, self.xc], self.own.at[3])

    def across(self, cps, own, core, start):
        def act(cp):
            if start:
                cp.start()
            else:
                cp.wait_send()
        for cp in cps[1:]:
            act(cp)

        @pl.when(self.c != core)
        def _():
            act(cps[0])
        if start:
            @pl.when(self.c == core)
            def _():
                own.start()

    def landed(self, src, dst, ss, rs, own, core):
        for i in range(NX):
            for k in range(NC):
                if i or k != core:
                    rcopy(src, dst, ss.at[0], rs.at[NC * i + k],
                          dev((self.x + 1) % NX, self.z, 1 - self.c, self.y)).wait_recv()
        own.wait()

    def start(self):
        self.across(self.b, self.b_own, 1, True)
        for cp in self.a:
            cp.start()
        self.a_own.start()

    def turn_b(self, lo, hi):
        @pl.when(self.c == 1)
        def _():
            if lo == 0:
                self.landed(self.s1.at[0], self.v.at[:, 0], self.bss, self.brs, self.b_own, 1)
            for cp in self.cc[lo:hi]:
                cp.start()
            if hi == NZ - 1:
                self.c_own.start()

    def turn_a(self):
        for cp in self.a:
            cp.wait_recv()
        self.a_own.wait()
        self.across(self.d, self.d_own, 0, True)

    def finish(self):
        @pl.when(self.c == 1)
        def _():
            for cp in self.cc:
                cp.wait_recv()
            self.c_own.wait()

        @pl.when(self.c == 0)
        def _():
            self.landed(self.u.at[:, 0], self.h.at[:, 0], self.dss, self.drs, self.d_own, 0)

    def sent(self):
        for cp in self.a:
            cp.wait_send()
        self.across(self.b, self.b_own, 1, False)
        self.across(self.d, self.d_own, 0, False)

        @pl.when(self.c == 1)
        def _():
            for cp in self.cc:
                cp.wait_send()


def layer_kernel(feats_hbm, ws_hbm, wn_hbm, cot_hbm, bias_ref, deg_ref, edge_ref, send_ref, hub_ref,
                 out_hbm, grad_hbm, btot_ref, wfull_ref,
                 fv, wsv, wnv, cotv, eslot, at, hown, zbuf, z32, hubtab, h_ref,
                 acc, pre0, dvs, nmv, glv, egv, fvt, out_v, base_v, grad_v, ret_ref, s0, s1, u, v, g0, g1, gu, gv,
                 hubg, wg, bg, hubc, wc, bc, hub1, w1, b1, hubp, wp, bp,
                 wn_s, wn_r, wf_s, wf_r, bn_s, bn_r, bf_s, bf_r, hz_s, hz_r,
                 in_sem, hz_ss, hz_rs, hp_ss, hp_rs, hc_ss, hc_rs,
                 c_ss, c_rs, p_ss, p_rs, q_ss, q_rs, n_ss, n_rs, f_ss, f_rs,
                 ap_ss, ap_rs, ac_ss, ac_rs, *ex_sems):
    x, z, c, y = coords()
    barrier, nbar = entry_barrier_signal(x, z, c, y)
    fwd = Exchange(s0, s1, u, v, h_ref, ex_sems[:9])
    bwd = Exchange(g0, g1, gu, gv, ret_ref, ex_sems[9:])
    yx = y * NX + x
    sib = dev(x, z, 1 - c, y)
    offs = z_offsets()
    zp = [((z + i) % NZ, dev(x, (z + i) % NZ, c, y)) for i in offs[:-1]]
    yxp = [(((y + i // NX) % NY) * NX + (x + i % NX) % NX, p)
           for i, p in enumerate(yx_peers(x, z, c, y), 1)]
    started = []

    def go(cps):
        for cp in cps:
            cp.start()
        started.extend(cps)
        return cps

    def flush_part(cps):
        for cp in cps:
            cp.wait_send()
        gone = {id(cp) for cp in cps}
        started[:] = [cp for cp in started if id(cp) not in gone]

    def flush():
        for cp in started:
            cp.wait_send()
        started.clear()

    def arrive(cps):
        for cp in cps:
            cp.wait_recv()

    def pass_on(cps, buf, ss, rs):
        out = go([rcopy(buf.at[c, yx], buf.at[c, yx], ss.at[0], rs.at[0], sib)])
        for i, cp in enumerate(cps, 1):
            cp.wait_recv()
            k = ((y + NY - i // NX) % NY) * NX + (x + NX - i % NX) % NX
            out += go([rcopy(buf.at[c, k], buf.at[c, k], ss.at[i], rs.at[i], sib)])
        return out

    rows, width = fv.shape
    fan = edge_ref.shape[0]
    slots = at.shape[0]
    hubs = 2 * NC * NYX * NZ
    halos = 4 * NXC * NZ
    loads = [pltpu.make_async_copy(src, dst, in_sem.at[i]) for i, (src, dst) in enumerate(
        ((feats_hbm, fv), (ws_hbm, wsv), (wn_hbm, wnv), (cot_hbm, cotv)))]
    for cp in loads:
        cp.start()

    stores = [pltpu.make_async_copy(out_v, out_hbm, in_sem.at[5]),
              pltpu.make_async_copy(grad_v, grad_hbm, in_sem.at[6])]

    half = halos // 2
    p = lax.broadcasted_iota(jnp.int32, (halos, 1), 0)
    p2 = div(mod(p, half), 4)
    want = jnp.where(p < half, (mod(p2, NX) * NZ + div(p2, NX)) * NC, p2 * NC + 1)
    ids = list_ids_column(send_ref, want)
    hot = jnp.where(ids == lax.broadcasted_iota(jnp.int32, (halos, rows), 1), 1.0, 0.0).astype(BF16)
    loads[0].wait()
    picked = jnp.dot(hot, fv[...], preferred_element_type=F32)
    s0[...] = picked[:half].reshape(s0.shape).astype(BF16)
    s1[...] = picked[half:].reshape(s1.shape).astype(BF16)
    sub = lax.broadcasted_iota(jnp.int32, (8, rows), 0)
    hrow = jnp.where(sub == 0, hub_ref[0], jnp.where(sub == 1, hub_ref[1], -1))
    hhot = jnp.where(hrow == lax.broadcasted_iota(jnp.int32, (8, rows), 1), 1.0, 0.0).astype(BF16)
    hown[...] = jnp.dot(hhot, fv[...], preferred_element_type=F32)[:2]

    e = edge_ref[...]
    h = e - rows
    hub_pos = (((mod(div(h, 2 * NY), NC) * NY + mod(div(h, 2), NY)) * NX
                + div(h, 2 * NY * NC * NZ)) * NZ + mod(div(h, 2 * NY * NC), NZ)) * 2 + mod(h, 2)
    g = h - hubs
    halo_pos = ((mod(div(g, 4 * NC), NZ) * NX + div(g, 4 * NC * NZ)) * NC + mod(div(g, 4), NC)) * 4 + mod(g, 4)
    pos = jnp.where(e < rows, e, jnp.where(e < rows + hubs, rows + hub_pos, rows + hubs + halo_pos))
    count = jnp.minimum(deg_ref[...], fan)
    live = lax.broadcasted_iota(jnp.int32, e.shape, 0) < count
    eslot[...] = jnp.where(live, pos, -1)
    nb = 128 if rows % 128 == 0 else 64
    i16 = jnp.int16

    def build(lo, hi):
        def body(j, carry):
            c0 = pl.multiple_of(j * nb, nb)
            sl = lax.broadcasted_iota(jnp.int32, (16, nb), 0)
            diff = [(jnp.broadcast_to(eslot[k:k + 1, pl.ds(c0, nb)], (16, nb)) - sl).astype(i16)
                    for k in range(fan)]
            for t in range(slots // 16):
                tot = None
                for k in range(fan):
                    one = jnp.where(diff[k] == i16(t * 16), BF16(1.0), BF16(0.0))
                    tot = one if tot is None else tot + one
                at[t * 16:(t + 1) * 16, pl.ds(c0, nb)] = tot
            return carry
        lax.fori_loop(lo, hi, body, 0)

    nblk = rows // nb
    cuts = [0, nblk // 8, nblk * 3 // 8, nblk * 5 // 8, nblk]

    zb = pltpu.make_async_copy(hown, zbuf.at[z], in_sem.at[4])
    zb.start()
    build(cuts[0], cuts[1])
    pl.semaphore_wait(barrier, nbar)
    hz = go([rcopy(hown, zbuf.at[z], hz_ss.at[i], hz_rs.at[i], d) for i, (k, d) in enumerate(zp)])
    fwd.start()
    build(cuts[1], cuts[2])
    fvt[...] = fv[...].T
    fwd.turn_b(0, NZ - 1)
    build(cuts[2], cuts[3])
    zb.wait()
    arrive(hz)
    for i in range(NZ):
        z32[2 * i:2 * i + 2, :] = zbuf[i]
    hubtab[c, yx] = z32[...].astype(BF16)
    hp = go([rcopy(hubtab.at[c, yx], hubtab.at[c, yx], hp_ss.at[i], hp_rs.at[i], d)
             for i, (k, d) in enumerate(yxp)])
    fwd.turn_a()
    build(cuts[3], cuts[4])
    acc[...] = jnp.dot(fvt[...], at[:rows, :], preferred_element_type=F32)
    for cp in loads[1:]:
        cp.wait()
    hc = pass_on(hp, hubtab, hc_ss, hc_rs)
    blk = min(256, rows)
    spans = [slice(b * blk, (b + 1) * blk) for b in range(rows // blk)]
    for rs in spans:
        pre0[rs, :] = jnp.dot(fv[rs, :], wsv[...], preferred_element_type=F32) + bias_ref[...]
    dvs[...] = 1.0 / lax.dot_general(jnp.where(live, 1.0, 0.0).astype(BF16),
                                     jnp.ones((fan, width), BF16), TN, preferred_element_type=F32)
    rvc = 1.0 / count.astype(F32)
    arrive(hc)
    hub_rows = hubtab[...].reshape(hubs, width)
    acc[...] += jnp.dot(hub_rows.T, at[rows:rows + hubs, :], preferred_element_type=F32)
    fwd.finish()

    halo = h_ref[...].reshape(halos, width).T
    bsum = jnp.zeros((1, width), F32)
    for rs in spans:
        summed = acc[:, rs] + jnp.dot(halo, at[rows + hubs:, rs], preferred_element_type=F32)
        nmt = (summed * rvc[:, rs]).astype(BF16)
        nmv[:, rs] = nmt
        pre = pre0[rs, :] + lax.dot_general(nmt, wnv[...], TN, preferred_element_type=F32)
        ex = jnp.exp(jnp.minimum(pre, 0.0))
        act = jnp.where(pre > 0, pre, ex - 1.0)
        inv = lax.rsqrt(jnp.mean(act * act, axis=-1, keepdims=True) + NORM_EPS)
        out_v[rs, :] = (act * inv).astype(BF16)
        cot = cotv[rs, :].astype(F32)
        dot = jnp.mean(act * cot, axis=-1, keepdims=True)
        gpre = inv * (cot - act * (inv * inv * dot)) * jnp.where(pre > 0, 1.0, ex)
        bsum = bsum + jnp.sum(gpre, axis=0, keepdims=True)
        glv[rs, :] = gpre.astype(BF16)
    bg[...] = bsum
    gl = glv[...]
    wrows = wg.shape[2]
    wg[...] = jnp.concatenate(
        [jnp.dot(fvt[...], gl, preferred_element_type=F32),
         jnp.dot(nmv[...], gl, preferred_element_type=F32)], axis=0).reshape(wg.shape)
    cw = go([rcopy(wg.at[1 - c], wc, c_ss.at[0], c_rs.at[0], sib)])
    cb = go([rcopy(bg, bc, c_ss.at[1], c_rs.at[1], sib)])
    stores[0].start()
    for rs in spans:
        egv[rs, :] = (lax.dot_general(glv[rs, :], wnv[...], NT, preferred_element_type=F32)
                      * dvs[rs, :]).astype(BF16)
    eg = egv[...]
    flush_part(hz + hp + hc)

    hub_grad = jnp.dot(at[rows:rows + hubs, :], eg, preferred_element_type=F32)
    hubg[...] = hub_grad.reshape(hubg.shape).astype(BF16)
    ch = go([rcopy(hubg.at[1 - c], hubc, c_ss.at[2], c_rs.at[2], sib)])
    halo_grad = jnp.dot(at[rows + hubs:, :], eg, preferred_element_type=F32)
    halo_grad = halo_grad.reshape(NZ, NX, NC, 4, width).astype(BF16)
    g0[...] = halo_grad[:, :, 0]
    for i in range(NX):
        g1[i] = halo_grad[:, i, 1]
    arrive(cw)
    w1[...] = (wg[c] + wc[...]).astype(BF16)
    pw = go([rcopy(w1.at[k], wp.at[i], p_ss.at[0, i], p_rs.at[0, i], d)
             for i, (k, d) in enumerate(yxp)])
    bwd.start()
    arrive(ch)
    hub1[...] = (hubg[c].astype(F32) + hubc[...].astype(F32)).astype(BF16)
    ph = go([rcopy(hub1.at[k], hubp.at[i], p_ss.at[2, i], p_rs.at[2, i], d)
             for i, (k, d) in enumerate(yxp)])
    arrive(cb)
    b1[...] = bg[...] + bc[...]
    pb = go([rcopy(b1, bp.at[i], p_ss.at[1, i], p_rs.at[1, i], d) for i, (k, d) in enumerate(yxp)])
    base_v[...] = (lax.dot_general(gl, wsv[...], NT, preferred_element_type=F32)
                   + jnp.dot(at[:rows, :], eg, preferred_element_type=F32))
    arrive(pw)
    w = w1[yx].astype(F32)
    for i in range(NYX - 1):
        w = w + wp[i].astype(F32)
    wn_s[...] = w
    zlo = z % NZL
    zn = [dev(x, z - zlo + (zlo + i) % NZL, c, y) for i in range(1, NZL)]
    near = go([rcopy(wn_s, wn_r.at[i], n_ss.at[0, i], n_rs.at[0, i], d) for i, d in enumerate(zn)])
    arrive(pb)
    bias = b1[...]
    for i in range(NYX - 1):
        bias = bias + bp[i]
    bn_s[...] = bias
    nearb = go([rcopy(bn_s, bn_r.at[i], n_ss.at[1, i], n_rs.at[1, i], d) for i, d in enumerate(zn)])
    arrive(ph)
    hub = hub1[yx].astype(F32)
    for i in range(NYX - 1):
        hub = hub + hubp[i].astype(F32)
    for i in range(NZ):
        hz_s[i] = hub[2 * i:2 * i + 2, :]
    zh = go([rcopy(hz_s.at[k], hz_r.at[j], q_ss.at[j], q_rs.at[j], d)
             for j, (k, d) in enumerate(zp)])
    arrive(near)
    for i in range(NZL - 1):
        w = w + wn_r[i]
    wf_s[...] = w.astype(BF16)
    zf = [dev(x, (z + NZL * i) % NZ, c, y) for i in range(1, NZ // NZL)]
    farz = go([rcopy(wf_s, wf_r.at[i], f_ss.at[0, i], f_rs.at[0, i], d) for i, d in enumerate(zf)])
    arrive(nearb)
    for i in range(NZL - 1):
        bias = bias + bn_r[i]
    bf_s[...] = bias
    farb = go([rcopy(bf_s, bf_r.at[i], f_ss.at[1, i], f_rs.at[1, i], d) for i, d in enumerate(zf)])
    bwd.turn_b(0, NZ - 1)
    bwd.turn_a()
    fwd.sent()
    pl_all = div(lax.broadcasted_iota(jnp.int32, (1, halos), 1), 4)
    hot = hot_nodes(list_ids(send_ref, (mod(div(pl_all, NC), NX) * NZ + div(pl_all, NXC)) * NC
                             + mod(pl_all, NC)), rows)
    arrive(farz)
    w = wf_s[...].astype(F32)
    for i in range(NZ // NZL - 1):
        w = w + wf_r[i].astype(F32)
    wfull_ref[c, yx] = w.astype(BF16)
    ap = go([rcopy(wfull_ref.at[c, yx], wfull_ref.at[c, yx], ap_ss.at[i], ap_rs.at[i], d)
             for i, (k, d) in enumerate(yxp)])
    arrive(farb)
    for i in range(NZ // NZL - 1):
        bias = bias + bf_r[i]
    btot_ref[...] = bias
    flush_part(ch + pw + ph + pb + near + nearb + farz + farb + zh + cb + cw)
    arrive(zh)
    own = hz_s[z]
    for j in range(NZ - 1):
        own = own + hz_r[j]
    bwd.finish()
    total = base_v[...] + jnp.dot(hot, ret_ref[...].reshape(halos, width), preferred_element_type=F32)
    row = lax.broadcasted_iota(jnp.int32, (rows, 1), 0)
    for i in range(2):
        total = total + jnp.where(row == hub_ref[i], own[i:i + 1, :], 0.0)
    grad_v[...] = total.astype(BF16)
    stores[1].start()
    ac = pass_on(ap, wfull_ref, ac_ss, ac_rs)
    arrive(ac)
    flush()
    bwd.sent()
    for cp in stores:
        cp.wait()


def final_kernel(outs_hbm, grad_hbm, btot_hbm, wfull_hbm,
                 out_hbm, gout_hbm, us_hbm, un_hbm, ub_hbm, ov, gv, bv, wv, us, un, ub, sem, rsem):
    width = bv.shape[1]
    loads = [pltpu.make_async_copy(a, b, sem.at[i]) for i, (a, b) in enumerate(
        ((wfull_hbm, wv), (btot_hbm, bv), (outs_hbm, ov), (grad_hbm, gv)))]
    stores = [pltpu.make_async_copy(a, b, rsem.at[i]) for i, (a, b) in enumerate(
        ((us, us_hbm), (un, un_hbm), (ub, ub_hbm), (ov, out_hbm), (gv, gout_hbm)))]
    for cp in loads:
        cp.start()
    loads[0].wait()
    w = wv[...].reshape(2 * width, width).astype(F32)
    for o, ref in ((0, us), (width, un)):
        part = w[o:o + width, :]
        ref[...] = part * lax.rsqrt(jnp.mean(part * part) + UNIT_EPS)
    loads[1].wait()
    bias = bv[...]
    ub[...] = bias * lax.rsqrt(jnp.mean(bias * bias) + UNIT_EPS)
    for st in stores[:3]:
        st.start()
    for cp, st in zip(loads[2:], stores[3:]):
        cp.wait()
        st.start()
    for st in stores:
        st.wait()


def vmem():
    return pl.BlockSpec(memory_space=pltpu.VMEM)


def sds(shape, dtype):
    return jax.ShapeDtypeStruct(shape, dtype)


LIMIT = 56 << 20


def on_device(feats, w_self, w_neigh, bias, out_cot, degree, edge_src, hub_rows, send_rows):
    rows, width = feats.shape
    hubs = 2 * NC * NYX * NZ
    halos = 4 * NXC * NZ
    slots = rows + hubs + halos
    fan = edge_src.shape[1]
    wrows = 2 * width // (NC * NYX)
    dma = pltpu.SemaphoreType.DMA
    smem = pl.BlockSpec(memory_space=pltpu.SMEM)
    hbm = pl.BlockSpec(memory_space=pl.ANY)

    def vb(*shape):
        return pltpu.VMEM(shape, BF16)

    def vf(*shape):
        return pltpu.VMEM(shape, F32)

    send_t = send_rows.T
    outputs, grad, btot, wfull = pl.pallas_call(
        layer_kernel,
        out_shape=(sds((rows, width), BF16), sds((rows, width), BF16), sds((1, width), F32),
                   sds((NC, NYX, wrows, width), BF16)),
        in_specs=[hbm] * 4 + [vmem()] * 4 + [smem], out_specs=(hbm,) * 2 + (vmem(),) * 2,
        scratch_shapes=[
            vb(rows, width), vb(width, width), vb(width, width), vb(rows, width),
            pltpu.VMEM((fan, rows), jnp.int32), vb(slots, rows),
            vf(2, width), vf(NZ, 2, width), vf(2 * NZ, width), vb(NC, NYX, 2 * NZ, width),
            vb(NZ, NXC, 4, width), vf(width, rows), vf(rows, width), vf(rows, width),
            vb(width, rows), vb(rows, width), vb(rows, width), vb(width, rows),
            vb(rows, width), vf(rows, width), vb(rows, width), vb(NZ, NXC, 4, width),
            *[vb(NZ, NX, 4, width), vb(NX, NZ, 4, width), vb(NZ, NX, 4, width),
              vb(NZ, NXC, 4, width)] * 2,
            vb(NC, NYX, 2 * NZ, width), vf(NC, NYX, wrows, width), vf(1, width),
            vb(NYX, 2 * NZ, width), vf(NYX, wrows, width), vf(1, width),
            vb(NYX, 2 * NZ, width), vb(NYX, wrows, width), vf(1, width),
            vb(NYX - 1, 2 * NZ, width), vb(NYX - 1, wrows, width), vf(NYX - 1, 1, width),
            vf(wrows, width), vf(NZL - 1, wrows, width),
            vb(wrows, width), vb(max(NZ // NZL - 1, 1), wrows, width),
            vf(1, width), vf(NZL - 1, 1, width), vf(1, width), vf(max(NZ // NZL - 1, 1), 1, width),
            vf(NZ, 2, width), vf(NZ - 1, 2, width),
            dma((7,)), dma((NZ - 1,)), dma((NZ - 1,)), dma((NYX - 1,)), dma((NYX - 1,)),
            dma((NYX,)), dma((NYX,)),
            dma((3,)), dma((3,)), dma((3, NYX - 1)), dma((3, NYX - 1)), dma((NZ - 1,)), dma((NZ - 1,)),
            dma((2, NZL - 1)), dma((2, NZL - 1)),
            dma((2, max(NZ // NZL - 1, 1))), dma((2, max(NZ // NZL - 1, 1))),
            dma((NYX - 1,)), dma((NYX - 1,)), dma((NYX,)), dma((NYX,)),
            *[dma((4,)), dma((NZ - 1,)), dma((NZ - 1,)), dma((NX,)), dma((NXC,)),
              dma((NZ - 1,)), dma((NZ - 1,)), dma((NX,)), dma((NXC,))] * 2],
        compiler_params=pltpu.CompilerParams(
            collective_id=0, has_side_effects=True, vmem_limit_bytes=LIMIT),
    )(feats, w_self, w_neigh, out_cot, bias.reshape(1, width), degree.reshape(1, rows), edge_src.T,
      send_t, hub_rows)

    outputs, grad, us, un, ub = pl.pallas_call(
        final_kernel,
        out_shape=(sds((rows, width), BF16), sds((rows, width), BF16), sds((width, width), F32),
                   sds((width, width), F32), sds((1, width), F32)),
        in_specs=[hbm] * 4, out_specs=(hbm,) * 5,
        scratch_shapes=[vb(rows, width), vb(rows, width), vf(1, width), vb(NC, NYX, wrows, width),
                        vf(width, width), vf(width, width), vf(1, width), dma((4,)), dma((5,))],
        compiler_params=pltpu.CompilerParams(vmem_limit_bytes=LIMIT),
    )(outputs, grad, btot, wfull)
    return outputs, grad, us, un, ub.reshape(width)


def solution(mesh):
    both = ("dom", "rep")
    placed = (P(both, None), P(), P(), P(), P(both, None), P(both), P(both, None), P(both),
              P(both, None))
    return jax.shard_map(
        on_device,
        mesh=mesh,
        in_specs=placed,
        out_specs=(P(both, None), P(both, None), P(), P(), P()),
        check_vma=False,
    )
```

```python
import jax
import jax.numpy as jnp
from jax import lax
from jax.experimental import pallas as pl
from jax.experimental.pallas import tpu as pltpu
from jax.sharding import PartitionSpec as P

NORM_EPS = 1e-05
UNIT_EPS = 1e-06
NX, NZ, NC, NY = 4, 16, 2, 4
NZL = 4
NYX = NY * NX
NXC = NX * NC
MESH = pl.DeviceIdType.MESH
F32 = jnp.float32
BF16 = jnp.bfloat16


def coords():
    d = lax.axis_index("dom")
    y = lax.axis_index("rep")
    return d // (NZ * NC), (d // NC) % NZ, d % NC, y


def dev(x, z, c, y):
    return ((x * NZ + z) * NC + c, y)


def z_offsets():
    return [NZ // 2 - (j + 1) // 2 if j % 2 else NZ // 2 + j // 2 for j in range(NZ)]


def z_peers(x, z, c, y):
    return [dev(x, (z + i) % NZ, c, y) for i in range(1, NZ)]


def yx_peers(x, z, c, y):
    return [dev((x + i % NX) % NX, z, c, (y + i // NX) % NY) for i in range(1, NYX)]


def xc_peers(x, z, c, y):
    return [dev((x + i // NC) % NX, z, (c + i % NC) % NC, y) for i in range(1, NXC)]


def entry_barrier_signal(x, z, c, y):
    peers = z_peers(x, z, c, y) + xc_peers(x, z, c, y)
    peers += [p for i, p in enumerate(yx_peers(x, z, c, y), 1) if i // NX != 0]
    barrier = pltpu.get_barrier_semaphore()
    for p in peers:
        pl.semaphore_signal(barrier, inc=1, device_id=p, device_id_type=MESH)
    return barrier, len(peers)


def rcopy(src, dst, ssem, rsem, peer):
    return pltpu.make_async_remote_copy(
        src_ref=src, dst_ref=dst, send_sem=ssem, recv_sem=rsem, device_id=peer, device_id_type=MESH
    )


TN = (((0,), (0,)), ((), ()))
NT = (((1,), (1,)), ((), ()))


def list_ids(send_ref, want):
    ids = send_ref[...]
    places, lists = ids.shape
    n = want.shape[1]
    pick = jnp.where(lax.broadcasted_iota(jnp.int32, (lists, n), 0) == want, 1.0, 0.0).astype(BF16)
    hi = jnp.dot((ids >> 5).astype(F32).astype(BF16), pick, preferred_element_type=F32)
    lo = jnp.dot((ids & 31).astype(F32).astype(BF16), pick, preferred_element_type=F32)
    place = lax.broadcasted_iota(jnp.int32, (places, n), 1) & 3
    mine = place == lax.broadcasted_iota(jnp.int32, (places, n), 0)
    return jnp.sum(jnp.where(mine, hi * 32.0 + lo, 0.0), axis=0, keepdims=True).astype(jnp.int32)


def list_ids_column(send_ref, want):
    ids = send_ref[...]
    places, lists = ids.shape
    n = want.shape[0]
    pick = jnp.where(lax.broadcasted_iota(jnp.int32, (n, lists), 1) == want, 1.0, 0.0).astype(BF16)
    both = jnp.concatenate([ids >> 5, ids & 31], axis=0).astype(F32).astype(BF16)
    got = lax.dot_general(pick, both, NT, preferred_element_type=F32)
    lane = lax.broadcasted_iota(jnp.int32, got.shape, 1)
    mine = (lax.broadcasted_iota(jnp.int32, got.shape, 0) & 3) == (lane & 3)
    got = jnp.where(lane < places, got * 32.0, got)
    return jnp.sum(jnp.where(mine, got, 0.0), axis=1, keepdims=True).astype(jnp.int32)


def div(v, n):
    return v >> (n.bit_length() - 1)


def mod(v, n):
    return v & (n - 1)


def hot_nodes(ids, rows):
    node = lax.broadcasted_iota(jnp.int32, (rows, 128 if ids.shape[1] % 128 == 0 else ids.shape[1]), 0)
    w = node.shape[1]
    return jnp.concatenate(
        [jnp.where(ids[:, o:o + w] == node, 1.0, 0.0).astype(BF16) for o in range(0, ids.shape[1], w)],
        axis=1)


class Exchange:
    def __init__(self, s0, s1, u, v, h, sems):
        self.s0, self.s1, self.u, self.v, self.h = s0, s1, u, v, h
        (self.own, self.ass, self.ars, self.bss, self.brs, self.css, self.crs, self.dss,
         self.drs) = sems
        self.x, self.z, self.c, self.y = coords()
        self.xc = self.x * NC + self.c
        x, z, c, y = self.x, self.z, self.c, self.y
        self.offs = z_offsets()
        self.zp = [((z + i) % NZ, dev(x, (z + i) % NZ, c, y)) for i in self.offs[:-1]]
        self.a = [rcopy(s0.at[k], u.at[z], self.ass.at[j], self.ars.at[j], d)
                  for j, (k, d) in enumerate(self.zp)]
        self.a_own = pltpu.make_async_copy(s0.at[z], u.at[z], self.own.at[0])
        self.cc = [rcopy(v.at[k], h.at[z], self.css.at[j], self.crs.at[j], d)
                   for j, (k, d) in enumerate(self.zp)]
        self.c_own = pltpu.make_async_copy(v.at[z], h.at[z], self.own.at[1])
        self.b = [rcopy(s1.at[(x + i) % NX], v.at[:, self.xc], self.bss.at[i],
                        self.brs.at[NC * i + c], dev((x + i) % NX, z, 1, y)) for i in range(NX)]
        self.b_own = pltpu.make_async_copy(s1.at[x], v.at[:, self.xc], self.own.at[2])
        self.d = [rcopy(u.at[:, (x + i) % NX], h.at[:, self.xc], self.dss.at[i],
                        self.drs.at[NC * i + c], dev((x + i) % NX, z, 0, y)) for i in range(NX)]
        self.d_own = pltpu.make_async_copy(u.at[:, x], h.at[:, self.xc], self.own.at[3])

    def across(self, cps, own, core, start):
        def act(cp):
            if start:
                cp.start()
            else:
                cp.wait_send()
        for cp in cps[1:]:
            act(cp)

        @pl.when(self.c != core)
        def _():
            act(cps[0])
        if start:
            @pl.when(self.c == core)
            def _():
                own.start()

    def landed(self, src, dst, ss, rs, own, core):
        for i in range(NX):
            for k in range(NC):
                if i or k != core:
                    rcopy(src, dst, ss.at[0], rs.at[NC * i + k],
                          dev((self.x + 1) % NX, self.z, 1 - self.c, self.y)).wait_recv()
        own.wait()

    def start(self):
        self.across(self.b, self.b_own, 1, True)
        for cp in self.a:
            cp.start()
        self.a_own.start()

    def turn_b(self, lo, hi):
        @pl.when(self.c == 1)
        def _():
            if lo == 0:
                self.landed(self.s1.at[0], self.v.at[:, 0], self.bss, self.brs, self.b_own, 1)
            for cp in self.cc[lo:hi]:
                cp.start()
            if hi == NZ - 1:
                self.c_own.start()

    def turn_a(self):
        for cp in self.a:
            cp.wait_recv()
        self.a_own.wait()
        self.across(self.d, self.d_own, 0, True)

    def finish(self):
        @pl.when(self.c == 1)
        def _():
            for cp in self.cc:
                cp.wait_recv()
            self.c_own.wait()

        @pl.when(self.c == 0)
        def _():
            self.landed(self.u.at[:, 0], self.h.at[:, 0], self.dss, self.drs, self.d_own, 0)

    def sent(self):
        for cp in self.a:
            cp.wait_send()
        self.across(self.b, self.b_own, 1, False)
        self.across(self.d, self.d_own, 0, False)

        @pl.when(self.c == 1)
        def _():
            for cp in self.cc:
                cp.wait_send()


def layer_kernel(feats_hbm, ws_hbm, wn_hbm, cot_hbm, bias_ref, deg_ref, edge_ref, send_ref, hub_ref,
                 out_hbm, grad_hbm, btot_ref, wfull_ref,
                 fv, wsv, wnv, cotv, eslot, at, hown, zbuf, z32, hubtab, h_ref,
                 acc, pre0, dvs, nmv, glv, egv, fvt, out_v, base_v, grad_v, ret_ref, s0, s1, u, v, g0, g1, gu, gv,
                 hubg, wg, bg, hubc, wc, bc, hub1, w1, b1, hubp, wp, bp,
                 wn_s, wn_r, wf_s, wf_r, bn_s, bn_r, bf_s, bf_r, hz_s, hz_r,
                 in_sem, hz_ss, hz_rs, hp_ss, hp_rs, hc_ss, hc_rs,
                 c_ss, c_rs, p_ss, p_rs, q_ss, q_rs, n_ss, n_rs, f_ss, f_rs,
                 ap_ss, ap_rs, ac_ss, ac_rs, *ex_sems):
    x, z, c, y = coords()
    barrier, nbar = entry_barrier_signal(x, z, c, y)
    fwd = Exchange(s0, s1, u, v, h_ref, ex_sems[:9])
    bwd = Exchange(g0, g1, gu, gv, ret_ref, ex_sems[9:])
    yx = y * NX + x
    sib = dev(x, z, 1 - c, y)
    offs = z_offsets()
    zp = [((z + i) % NZ, dev(x, (z + i) % NZ, c, y)) for i in offs[:-1]]
    yxp = [(((y + i // NX) % NY) * NX + (x + i % NX) % NX, p)
           for i, p in enumerate(yx_peers(x, z, c, y), 1)]
    started = []

    def go(cps):
        for cp in cps:
            cp.start()
        started.extend(cps)
        return cps

    def flush_part(cps):
        for cp in cps:
            cp.wait_send()
        gone = {id(cp) for cp in cps}
        started[:] = [cp for cp in started if id(cp) not in gone]

    def flush():
        for cp in started:
            cp.wait_send()
        started.clear()

    def arrive(cps):
        for cp in cps:
            cp.wait_recv()

    def pass_on(cps, buf, ss, rs):
        out = go([rcopy(buf.at[c, yx], buf.at[c, yx], ss.at[0], rs.at[0], sib)])
        for i, cp in enumerate(cps, 1):
            cp.wait_recv()
            k = ((y + NY - i // NX) % NY) * NX + (x + NX - i % NX) % NX
            out += go([rcopy(buf.at[c, k], buf.at[c, k], ss.at[i], rs.at[i], sib)])
        return out

    rows, width = fv.shape
    fan = edge_ref.shape[0]
    slots = at.shape[0]
    hubs = 2 * NC * NYX * NZ
    halos = 4 * NXC * NZ
    loads = [pltpu.make_async_copy(src, dst, in_sem.at[i]) for i, (src, dst) in enumerate(
        ((feats_hbm, fv), (ws_hbm, wsv), (wn_hbm, wnv), (cot_hbm, cotv)))]
    for cp in loads:
        cp.start()

    stores = [pltpu.make_async_copy(out_v, out_hbm, in_sem.at[5]),
              pltpu.make_async_copy(grad_v, grad_hbm, in_sem.at[6])]

    half = halos // 2
    p = lax.broadcasted_iota(jnp.int32, (halos, 1), 0)
    p2 = div(mod(p, half), 4)
    want = jnp.where(p < half, (mod(p2, NX) * NZ + div(p2, NX)) * NC, p2 * NC + 1)
    ids = list_ids_column(send_ref, want)
    hot = jnp.where(ids == lax.broadcasted_iota(jnp.int32, (halos, rows), 1), 1.0, 0.0).astype(BF16)
    loads[0].wait()
    picked = jnp.dot(hot, fv[...], preferred_element_type=F32)
    s0[...] = picked[:half].reshape(s0.shape).astype(BF16)
    s1[...] = picked[half:].reshape(s1.shape).astype(BF16)
    sub = lax.broadcasted_iota(jnp.int32, (8, rows), 0)
    hrow = jnp.where(sub == 0, hub_ref[0], jnp.where(sub == 1, hub_ref[1], -1))
    hhot = jnp.where(hrow == lax.broadcasted_iota(jnp.int32, (8, rows), 1), 1.0, 0.0).astype(BF16)
    hown[...] = jnp.dot(hhot, fv[...], preferred_element_type=F32)[:2]

    e = edge_ref[...]
    h = e - rows
    hub_pos = (((mod(div(h, 2 * NY), NC) * NY + mod(div(h, 2), NY)) * NX
                + div(h, 2 * NY * NC * NZ)) * NZ + mod(div(h, 2 * NY * NC), NZ)) * 2 + mod(h, 2)
    g = h - hubs
    halo_pos = ((mod(div(g, 4 * NC), NZ) * NX + div(g, 4 * NC * NZ)) * NC + mod(div(g, 4), NC)) * 4 + mod(g, 4)
    pos = jnp.where(e < rows, e, jnp.where(e < rows + hubs, rows + hub_pos, rows + hubs + halo_pos))
    count = jnp.minimum(deg_ref[...], fan)
    live = lax.broadcasted_iota(jnp.int32, e.shape, 0) < count
    eslot[...] = jnp.where(live, pos, -1)
    nb = 128 if rows % 128 == 0 else 64
    i16 = jnp.int16

    def build(lo, hi):
        def body(j, carry):
            c0 = pl.multiple_of(j * nb, nb)
            sl = lax.broadcasted_iota(jnp.int32, (16, nb), 0)
            diff = [(jnp.broadcast_to(eslot[k:k + 1, pl.ds(c0, nb)], (16, nb)) - sl).astype(i16)
                    for k in range(fan)]
            for t in range(slots // 16):
                tot = None
                for k in range(fan):
                    one = jnp.where(diff[k] == i16(t * 16), BF16(1.0), BF16(0.0))
                    tot = one if tot is None else tot + one
                at[t * 16:(t + 1) * 16, pl.ds(c0, nb)] = tot
            return carry
        lax.fori_loop(lo, hi, body, 0)

    nblk = rows // nb
    cuts = [0, nblk // 8, nblk * 3 // 8, nblk * 5 // 8, nblk]

    zb = pltpu.make_async_copy(hown, zbuf.at[z], in_sem.at[4])
    zb.start()
    build(cuts[0], cuts[1])
    pl.semaphore_wait(barrier, nbar)
    hz = go([rcopy(hown, zbuf.at[z], hz_ss.at[i], hz_rs.at[i], d) for i, (k, d) in enumerate(zp)])
    fwd.start()
    build(cuts[1], cuts[2])
    fvt[...] = fv[...].T
    fwd.turn_b(0, NZ - 1)
    build(cuts[2], cuts[3])
    zb.wait()
    arrive(hz)
    for i in range(NZ):
        z32[2 * i:2 * i + 2, :] = zbuf[i]
    hubtab[c, yx] = z32[...].astype(BF16)
    hp = go([rcopy(hubtab.at[c, yx], hubtab.at[c, yx], hp_ss.at[i], hp_rs.at[i], d)
             for i, (k, d) in enumerate(yxp)])
    fwd.turn_a()
    build(cuts[3], cuts[4])
    acc[...] = jnp.dot(fvt[...], at[:rows, :], preferred_element_type=F32)
    for cp in loads[1:]:
        cp.wait()
    hc = pass_on(hp, hubtab, hc_ss, hc_rs)
    blk = min(256, rows)
    spans = [slice(b * blk, (b + 1) * blk) for b in range(rows // blk)]
    for rs in spans:
        pre0[rs, :] = jnp.dot(fv[rs, :], wsv[...], preferred_element_type=F32) + bias_ref[...]
    dvs[...] = 1.0 / lax.dot_general(jnp.where(live, 1.0, 0.0).astype(BF16),
                                     jnp.ones((fan, width), BF16), TN, preferred_element_type=F32)
    rvc = 1.0 / count.astype(F32)
    arrive(hc)
    hub_rows = hubtab[...].reshape(hubs, width)
    acc[...] += jnp.dot(hub_rows.T, at[rows:rows + hubs, :], preferred_element_type=F32)
    fwd.finish()

    halo = h_ref[...].reshape(halos, width).T
    bsum = jnp.zeros((1, width), F32)
    for rs in spans:
        summed = acc[:, rs] + jnp.dot(halo, at[rows + hubs:, rs], preferred_element_type=F32)
        nmt = (summed * rvc[:, rs]).astype(BF16)
        nmv[:, rs] = nmt
        pre = pre0[rs, :] + lax.dot_general(nmt, wnv[...], TN, preferred_element_type=F32)
        ex = jnp.exp(jnp.minimum(pre, 0.0))
        act = jnp.where(pre > 0, pre, ex - 1.0)
        inv = lax.rsqrt(jnp.mean(act * act, axis=-1, keepdims=True) + NORM_EPS)
        out_v[rs, :] = (act * inv).astype(BF16)
        cot = cotv[rs, :].astype(F32)
        dot = jnp.mean(act * cot, axis=-1, keepdims=True)
        gpre = inv * (cot - act * (inv * inv * dot)) * jnp.where(pre > 0, 1.0, ex)
        bsum = bsum + jnp.sum(gpre, axis=0, keepdims=True)
        glv[rs, :] = gpre.astype(BF16)
    bg[...] = bsum
    gl = glv[...]
    wrows = wg.shape[2]
    wg[...] = jnp.concatenate(
        [jnp.dot(fvt[...], gl, preferred_element_type=F32),
         jnp.dot(nmv[...], gl, preferred_element_type=F32)], axis=0).reshape(wg.shape)
    cw = go([rcopy(wg.at[1 - c], wc, c_ss.at[0], c_rs.at[0], sib)])
    cb = go([rcopy(bg, bc, c_ss.at[1], c_rs.at[1], sib)])
    stores[0].start()
    for rs in spans:
        egv[rs, :] = (lax.dot_general(glv[rs, :], wnv[...], NT, preferred_element_type=F32)
                      * dvs[rs, :]).astype(BF16)
    eg = egv[...]

    hub_grad = jnp.dot(at[rows:rows + hubs, :], eg, preferred_element_type=F32)
    hubg[...] = hub_grad.reshape(hubg.shape).astype(BF16)
    ch = go([rcopy(hubg.at[1 - c], hubc, c_ss.at[2], c_rs.at[2], sib)])
    halo_grad = jnp.dot(at[rows + hubs:, :], eg, preferred_element_type=F32)
    halo_grad = halo_grad.reshape(NZ, NX, NC, 4, width).astype(BF16)
    g0[...] = halo_grad[:, :, 0]
    for i in range(NX):
        g1[i] = halo_grad[:, i, 1]
    arrive(cw)
    w1[...] = (wg[c] + wc[...]).astype(BF16)
    pw = go([rcopy(w1.at[k], wp.at[i], p_ss.at[0, i], p_rs.at[0, i], d)
             for i, (k, d) in enumerate(yxp)])
    bwd.start()
    arrive(ch)
    hub1[...] = (hubg[c].astype(F32) + hubc[...].astype(F32)).astype(BF16)
    ph = go([rcopy(hub1.at[k], hubp.at[i], p_ss.at[2, i], p_rs.at[2, i], d)
             for i, (k, d) in enumerate(yxp)])
    arrive(cb)
    b1[...] = bg[...] + bc[...]
    pb = go([rcopy(b1, bp.at[i], p_ss.at[1, i], p_rs.at[1, i], d) for i, (k, d) in enumerate(yxp)])
    base_v[...] = (lax.dot_general(gl, wsv[...], NT, preferred_element_type=F32)
                   + jnp.dot(at[:rows, :], eg, preferred_element_type=F32))
    arrive(pw)
    w = w1[yx].astype(F32)
    for i in range(NYX - 1):
        w = w + wp[i].astype(F32)
    wn_s[...] = w
    zlo = z % NZL
    zn = [dev(x, z - zlo + (zlo + i) % NZL, c, y) for i in range(1, NZL)]
    near = go([rcopy(wn_s, wn_r.at[i], n_ss.at[0, i], n_rs.at[0, i], d) for i, d in enumerate(zn)])
    arrive(pb)
    bias = b1[...]
    for i in range(NYX - 1):
        bias = bias + bp[i]
    bn_s[...] = bias
    nearb = go([rcopy(bn_s, bn_r.at[i], n_ss.at[1, i], n_rs.at[1, i], d) for i, d in enumerate(zn)])
    arrive(ph)
    hub = hub1[yx].astype(F32)
    for i in range(NYX - 1):
        hub = hub + hubp[i].astype(F32)
    for i in range(NZ):
        hz_s[i] = hub[2 * i:2 * i + 2, :]
    zh = go([rcopy(hz_s.at[k], hz_r.at[j], q_ss.at[j], q_rs.at[j], d)
             for j, (k, d) in enumerate(zp)])
    arrive(near)
    for i in range(NZL - 1):
        w = w + wn_r[i]
    wf_s[...] = w.astype(BF16)
    zf = [dev(x, (z + NZL * i) % NZ, c, y) for i in range(1, NZ // NZL)]
    farz = go([rcopy(wf_s, wf_r.at[i], f_ss.at[0, i], f_rs.at[0, i], d) for i, d in enumerate(zf)])
    arrive(nearb)
    for i in range(NZL - 1):
        bias = bias + bn_r[i]
    bf_s[...] = bias
    farb = go([rcopy(bf_s, bf_r.at[i], f_ss.at[1, i], f_rs.at[1, i], d) for i, d in enumerate(zf)])
    bwd.turn_b(0, NZ - 1)
    bwd.turn_a()
    fwd.sent()
    pl_all = div(lax.broadcasted_iota(jnp.int32, (1, halos), 1), 4)
    hot = hot_nodes(list_ids(send_ref, (mod(div(pl_all, NC), NX) * NZ + div(pl_all, NXC)) * NC
                             + mod(pl_all, NC)), rows)
    flush_part(hz + hp + hc + cw + cb + ch + pw + ph + pb + near + nearb)
    arrive(farz)
    w = wf_s[...].astype(F32)
    for i in range(NZ // NZL - 1):
        w = w + wf_r[i].astype(F32)
    wfull_ref[c, yx] = w.astype(BF16)
    ap = go([rcopy(wfull_ref.at[c, yx], wfull_ref.at[c, yx], ap_ss.at[i], ap_rs.at[i], d)
             for i, (k, d) in enumerate(yxp)])
    arrive(farb)
    for i in range(NZ // NZL - 1):
        bias = bias + bf_r[i]
    btot_ref[...] = bias
    arrive(zh)
    own = hz_s[z]
    for j in range(NZ - 1):
        own = own + hz_r[j]
    bwd.finish()
    total = base_v[...] + jnp.dot(hot, ret_ref[...].reshape(halos, width), preferred_element_type=F32)
    row = lax.broadcasted_iota(jnp.int32, (rows, 1), 0)
    for i in range(2):
        total = total + jnp.where(row == hub_ref[i], own[i:i + 1, :], 0.0)
    grad_v[...] = total.astype(BF16)
    stores[1].start()
    ac = pass_on(ap, wfull_ref, ac_ss, ac_rs)
    arrive(ac)
    flush()
    bwd.sent()
    for cp in stores:
        cp.wait()


def final_kernel(outs_hbm, grad_hbm, btot_hbm, wfull_hbm,
                 out_hbm, gout_hbm, us_hbm, un_hbm, ub_hbm, ov, gv, bv, wv, us, un, ub, sem, rsem):
    width = bv.shape[1]
    loads = [pltpu.make_async_copy(a, b, sem.at[i]) for i, (a, b) in enumerate(
        ((wfull_hbm, wv), (btot_hbm, bv), (outs_hbm, ov), (grad_hbm, gv)))]
    stores = [pltpu.make_async_copy(a, b, rsem.at[i]) for i, (a, b) in enumerate(
        ((us, us_hbm), (un, un_hbm), (ub, ub_hbm), (ov, out_hbm), (gv, gout_hbm)))]
    for cp in loads:
        cp.start()
    loads[0].wait()
    w = wv[...].reshape(2 * width, width).astype(F32)
    for o, ref in ((0, us), (width, un)):
        part = w[o:o + width, :]
        ref[...] = part * lax.rsqrt(jnp.mean(part * part) + UNIT_EPS)
    loads[1].wait()
    bias = bv[...]
    ub[...] = bias * lax.rsqrt(jnp.mean(bias * bias) + UNIT_EPS)
    for st in stores[:3]:
        st.start()
    for cp, st in zip(loads[2:], stores[3:]):
        cp.wait()
        st.start()
    for st in stores:
        st.wait()


def vmem():
    return pl.BlockSpec(memory_space=pltpu.VMEM)


def sds(shape, dtype):
    return jax.ShapeDtypeStruct(shape, dtype)


LIMIT = 56 << 20


def on_device(feats, w_self, w_neigh, bias, out_cot, degree, edge_src, hub_rows, send_rows):
    rows, width = feats.shape
    hubs = 2 * NC * NYX * NZ
    halos = 4 * NXC * NZ
    slots = rows + hubs + halos
    fan = edge_src.shape[1]
    wrows = 2 * width // (NC * NYX)
    dma = pltpu.SemaphoreType.DMA
    smem = pl.BlockSpec(memory_space=pltpu.SMEM)
    hbm = pl.BlockSpec(memory_space=pl.ANY)

    def vb(*shape):
        return pltpu.VMEM(shape, BF16)

    def vf(*shape):
        return pltpu.VMEM(shape, F32)

    send_t = send_rows.T
    outputs, grad, btot, wfull = pl.pallas_call(
        layer_kernel,
        out_shape=(sds((rows, width), BF16), sds((rows, width), BF16), sds((1, width), F32),
                   sds((NC, NYX, wrows, width), BF16)),
        in_specs=[hbm] * 4 + [vmem()] * 4 + [smem], out_specs=(hbm,) * 2 + (vmem(),) * 2,
        scratch_shapes=[
            vb(rows, width), vb(width, width), vb(width, width), vb(rows, width),
            pltpu.VMEM((fan, rows), jnp.int32), vb(slots, rows),
            vf(2, width), vf(NZ, 2, width), vf(2 * NZ, width), vb(NC, NYX, 2 * NZ, width),
            vb(NZ, NXC, 4, width), vf(width, rows), vf(rows, width), vf(rows, width),
            vb(width, rows), vb(rows, width), vb(rows, width), vb(width, rows),
            vb(rows, width), vf(rows, width), vb(rows, width), vb(NZ, NXC, 4, width),
            *[vb(NZ, NX, 4, width), vb(NX, NZ, 4, width), vb(NZ, NX, 4, width),
              vb(NZ, NXC, 4, width)] * 2,
            vb(NC, NYX, 2 * NZ, width), vf(NC, NYX, wrows, width), vf(1, width),
            vb(NYX, 2 * NZ, width), vf(NYX, wrows, width), vf(1, width),
            vb(NYX, 2 * NZ, width), vb(NYX, wrows, width), vf(1, width),
            vb(NYX - 1, 2 * NZ, width), vb(NYX - 1, wrows, width), vf(NYX - 1, 1, width),
            vf(wrows, width), vf(NZL - 1, wrows, width),
            vb(wrows, width), vb(max(NZ // NZL - 1, 1), wrows, width),
            vf(1, width), vf(NZL - 1, 1, width), vf(1, width), vf(max(NZ // NZL - 1, 1), 1, width),
            vf(NZ, 2, width), vf(NZ - 1, 2, width),
            dma((7,)), dma((NZ - 1,)), dma((NZ - 1,)), dma((NYX - 1,)), dma((NYX - 1,)),
            dma((NYX,)), dma((NYX,)),
            dma((3,)), dma((3,)), dma((3, NYX - 1)), dma((3, NYX - 1)), dma((NZ - 1,)), dma((NZ - 1,)),
            dma((2, NZL - 1)), dma((2, NZL - 1)),
            dma((2, max(NZ // NZL - 1, 1))), dma((2, max(NZ // NZL - 1, 1))),
            dma((NYX - 1,)), dma((NYX - 1,)), dma((NYX,)), dma((NYX,)),
            *[dma((4,)), dma((NZ - 1,)), dma((NZ - 1,)), dma((NX,)), dma((NXC,)),
              dma((NZ - 1,)), dma((NZ - 1,)), dma((NX,)), dma((NXC,))] * 2],
        compiler_params=pltpu.CompilerParams(
            collective_id=0, has_side_effects=True, vmem_limit_bytes=LIMIT),
    )(feats, w_self, w_neigh, out_cot, bias.reshape(1, width), degree.reshape(1, rows), edge_src.T,
      send_t, hub_rows)

    outputs, grad, us, un, ub = pl.pallas_call(
        final_kernel,
        out_shape=(sds((rows, width), BF16), sds((rows, width), BF16), sds((width, width), F32),
                   sds((width, width), F32), sds((1, width), F32)),
        in_specs=[hbm] * 4, out_specs=(hbm,) * 5,
        scratch_shapes=[vb(rows, width), vb(rows, width), vf(1, width), vb(NC, NYX, wrows, width),
                        vf(width, width), vf(width, width), vf(1, width), dma((4,)), dma((5,))],
        compiler_params=pltpu.CompilerParams(vmem_limit_bytes=LIMIT),
    )(outputs, grad, btot, wfull)
    return outputs, grad, us, un, ub.reshape(width)


def solution(mesh):
    both = ("dom", "rep")
    placed = (P(both, None), P(), P(), P(), P(both, None), P(both), P(both, None), P(both),
              P(both, None))
    return jax.shard_map(
        on_device,
        mesh=mesh,
        in_specs=placed,
        out_specs=(P(both, None), P(both, None), P(), P(), P()),
        check_vma=False,
    )
```
